256 devices in a mesh: win: 16 (over z_hi, y), tmpl: 16 (over z_lo, x, core).
Axes of the slice: x: 4, y: 4, z: 8 (z_hi: 4, z_lo: 2; z = z_hi * 2 + z_lo), core: 2. Of those that a mesh axis runs over, the one named last changes fastest.
Arguments:
- raw: bfloat16 [4096, 32768], P(('win', 'tmpl')), may hold values from -160 to 160
- ids: int32 [4096], replicated, may hold values from -1 to 2447, as said below
- fir: bfloat16 [64], replicated, may hold values from -0.75 to 0.75
- taps: bfloat16 [2048, 30, 400], P('tmpl'), may hold values from -0.3125 to 0.3125
- channels: int32 [2048, 30], P('tmpl'), may hold values from 0 to 2447, all different within a row
- shifts: int32 [2048, 30], P('tmpl'), may hold values from 0 to 255
Outputs:
- stack: float32 [2048, 16384], P('tmpl', 'win')
The draws below stay inside these ranges and needn't reach their ends.
Inputs may be any that keep to these rules, and one draw needn't show every extreme that they name: `ids`: each station channel 0 to 2447 stands in exactly one slot, the others hold -1; the owners of one index of tmpl hold exactly 153 live slots together, and one owner of each holds 16 live slots. Each template names 30 different channels; every channel is named by some template.
All inputs are finite; a program needn't handle non-finite values.
Results may differ from the reference program's by a relative error of at most 0.007.
Values may be sent and summed in bfloat16 or wider, within the bound.
A program may use at most 128 MiB of HBM per device.

```python
import math
import jax
import jax.numpy as jnp
from jax import lax

WIN_DEV = 1024
MARGIN = 768
TL = 400
CH = 30
DEC = 2
NTAP = 64
MOVE = 256
SLOTS = 16
NS = 1792
NF = 896
NCHAN = 2448
ROWS_ALL = 4096
RAW_T = 32768
TEMPLATES = 2048
TIMES = 16384
N_WIN = 16
N_TMPL = 16


def draw_raw(key, part):
    noise_key, row_key, envelope_key = jax.random.split(key, 3)
    base = jnp.clip(jax.random.normal(noise_key, (ROWS_ALL, RAW_T), jnp.float32), -4.0, 4.0)
    row_scale = jnp.exp(jax.random.uniform(row_key, (ROWS_ALL, 1), jnp.float32, 0.0, math.log(10.0)))
    envelope = jnp.exp(jax.random.uniform(envelope_key, (ROWS_ALL, RAW_T // 64, 1), jnp.float32, 0.0, math.log(4.0)))
    shaped = (base.reshape(ROWS_ALL, RAW_T // 64, 64) * envelope).reshape(ROWS_ALL, RAW_T)
    return (shaped * row_scale).astype(jnp.bfloat16)


def draw_ids(key, part):
    column_count = N_WIN * SLOTS
    live_col = 3 * SLOTS * N_WIN // 5

    def column(subkey):
        owner_key, rank_key = jax.random.split(subkey)
        owner = jax.random.randint(owner_key, (), 0, N_WIN)
        slot_owner = jnp.arange(column_count, dtype=jnp.int32) // SLOTS
        ranking = jax.random.permutation(rank_key, column_count).astype(jnp.int32)
        score = jnp.where(slot_owner == owner, -1, ranking)
        ordering = jnp.argsort(score, stable=True)
        placing = jnp.argsort(ordering)
        return placing < live_col
    column_keys = jax.random.split(jax.random.fold_in(key, 7), N_TMPL)
    live = jax.vmap(column)(column_keys)
    live = live.reshape(N_TMPL, N_WIN, SLOTS).transpose(1, 0, 2).reshape(-1)
    channel_perm = jax.random.permutation(jax.random.fold_in(key, 11), NCHAN).astype(jnp.int32)
    counter = jnp.cumsum(live.astype(jnp.int32)) - 1
    picked = jnp.take(channel_perm, jnp.clip(counter, 0, NCHAN - 1))
    return jnp.where(live, picked, -1).astype(jnp.int32)


def with_ends(entries, rng, least, top_value):
    longest = entries.shape.index(max(entries.shape))
    spots = []
    for shift in (0, 1):
        where = [jax.random.randint(jax.random.fold_in(rng, axis), (), 0, length) for axis, length in enumerate(entries.shape)]
        where[longest] = (where[longest] + shift) % entries.shape[longest]
        spots.append(tuple(where))
    return entries.at[spots[0]].set(least).at[spots[1]].set(top_value)


def level_of(own_key, shape, cuts, smallest, largest):
    factor_of, own = 1.0, jax.random.fold_in(own_key, 6)
    for dim, parts in cuts:
        draws = jnp.exp(jax.random.uniform(jax.random.fold_in(own, dim), (parts,), jnp.float32, smallest / len(cuts), largest / len(cuts)))
        factor_of = factor_of * jnp.repeat(draws, shape[dim] // parts).reshape([-1 if axis == dim else 1 for axis in range(len(shape))])
    return factor_of


def different_ones(own_key, rows, number_of, top, lift):
    sequence = jax.random.permutation(jax.random.fold_in(own_key, 1), number_of)
    pull = sequence
    for power in range(3):
        pull = pull * pull // number_of
    pull = pull * lift // number_of
    tickets = jax.random.randint(jax.random.fold_in(own_key, 2), (rows, number_of), 0, 4096) + pull
    sure = jax.random.permutation(jax.random.fold_in(own_key, 3), rows)[jnp.arange(number_of) % rows]
    tickets = jnp.where(jnp.arange(rows)[:, None] == sure[None, :], 1 << 14, tickets)
    score = tickets * number_of + jnp.arange(number_of)
    return lax.top_k(score.astype(jnp.int32), top)[1].astype(jnp.int32)


def gaussian(stream_key, dims, scale, limit, cuts=(), kind=jnp.bfloat16):
    drawn = jax.random.normal(stream_key, dims, jnp.float32) * scale
    if len(cuts) > 0:
        drawn = level_of(stream_key, dims, cuts, -0.22, 0.18) * drawn
    return jnp.clip(drawn, min=-limit, max=limit).astype(kind)


def setup_inputs(seed: int = 0) -> dict:
    key_list = jax.random.split(jax.random.key(seed), 7)
    return {
        "raw": draw_raw(jax.random.fold_in(key_list[6], 71), 0),
        "ids": draw_ids(jax.random.fold_in(key_list[6], 71), 0),
        "fir": gaussian(key_list[2], (NTAP,), NTAP ** -0.5, 0.75),
        "taps": gaussian(key_list[3], (TEMPLATES, CH, TL), TL ** -0.5, 0.3125, ((0, 16),)),
        "channels": different_ones(key_list[4], TEMPLATES, NCHAN, CH, 100),
        "shifts": with_ends(jax.random.randint(key_list[5], (TEMPLATES, CH), 0, MOVE), jax.random.fold_in(key_list[5], 1), 0, MOVE - 1).astype(jnp.int32),
    }


def band_matrix(fir, block):
    in_index = jnp.arange(DEC * block + NTAP, dtype=jnp.int32)[:, None]
    out_index = jnp.arange(block, dtype=jnp.int32)[None, :]
    offset = in_index - DEC * out_index
    onehot = offset[:, :, None] == jnp.arange(NTAP, dtype=jnp.int32)[None, None, :]
    values = jnp.where(onehot, fir.astype(jnp.float32)[None, None, :], jnp.float32(0.0))
    return lax.optimization_barrier(jnp.sum(values, axis=2)).astype(jnp.bfloat16)

def decimate(raw_ext, fir, count):
    block = math.gcd(count, 128)
    pieces = count // block
    length = DEC * block
    height = raw_ext.shape[0]
    padded = jnp.pad(raw_ext, ((0, 0), (0, (pieces + 1) * length - raw_ext.shape[1])))
    blocks = padded.reshape(height, pieces + 1, length)
    segments = jnp.concatenate([blocks[:, :pieces], blocks[:, 1:, :NTAP]], axis=2)
    band = band_matrix(fir, block)
    result = jnp.einsum('rbi,in->rbn', segments, band, preferred_element_type=jnp.float32)
    return result.reshape(height, count)

def forward_table():
    sample_index = jnp.arange(NS, dtype=jnp.int32)[:, None]
    frequency = jnp.arange(NF, dtype=jnp.int32)[None, :]
    angle = (sample_index * frequency % NS).astype(jnp.float32) * jnp.float32(2.0 * math.pi / NS)
    return jnp.concatenate([jnp.cos(angle), jnp.sin(angle)], axis=1).astype(jnp.bfloat16)

def inverse_table():
    frequency = jnp.arange(NF, dtype=jnp.int32)[:, None]
    time_index = jnp.arange(WIN_DEV, dtype=jnp.int32)[None, :]
    angle = (frequency * time_index % NS).astype(jnp.float32) * jnp.float32(2.0 * math.pi / NS)
    return jnp.concatenate([jnp.cos(angle), -jnp.sin(angle)], axis=0).astype(jnp.bfloat16)

def spectra(tiles, table):
    values = tiles.astype(jnp.float32)
    scale = lax.rsqrt(lax.optimization_barrier(jnp.mean(values * values, axis=1, keepdims=True)) + 1e-05)
    return (jnp.dot(tiles, table, preferred_element_type=jnp.float32) * scale).astype(jnp.bfloat16)

def stack_block(template_spec, data_spec, shift_block, inverse):
    tmpl_cos = template_spec[:, :NF].astype(jnp.float32)
    tmpl_sin = template_spec[:, NF:].astype(jnp.float32)
    data_cos = data_spec[:, :NF].astype(jnp.float32)
    data_sin = data_spec[:, NF:].astype(jnp.float32)
    real_part = tmpl_cos * data_cos + tmpl_sin * data_sin
    imag_part = tmpl_sin * data_cos - tmpl_cos * data_sin
    frequency = jnp.arange(NF, dtype=jnp.int32)[None, :]
    angle = (shift_block[:, None] * frequency % NS).astype(jnp.float32) * jnp.float32(2.0 * math.pi / NS)
    phase_cos = jnp.cos(angle)
    phase_sin = jnp.sin(angle)
    rotated_real = real_part * phase_cos - imag_part * phase_sin
    rotated_imag = real_part * phase_sin + imag_part * phase_cos
    group = shift_block.shape[0] // CH
    summed_real = lax.optimization_barrier(jnp.sum(rotated_real.reshape(group, CH, NF), axis=1))
    summed_imag = lax.optimization_barrier(jnp.sum(rotated_imag.reshape(group, CH, NF), axis=1))
    weight = jnp.where(jnp.arange(NF) == 0, 1.0, 2.0).astype(jnp.float32) / jnp.float32(CH * NS)
    packed = jnp.concatenate([summed_real * weight, summed_imag * weight], axis=1).astype(jnp.bfloat16)
    return jnp.dot(packed, inverse, preferred_element_type=jnp.float32)

def reference(raw, ids, fir, taps, channels, shifts):
    whole = jnp.pad(raw, ((0, 0), (0, NTAP)))
    filtered = decimate(whole, fir, TIMES).astype(jnp.bfloat16)
    position = jnp.arange(ROWS_ALL, dtype=jnp.int32)
    keyed = jnp.where(ids >= 0, ids, NCHAN + position)
    row_of = jnp.argsort(keyed)[:NCHAN].astype(jnp.int32)
    by_channel = jnp.take(filtered, row_of, axis=0)
    padded = jnp.pad(by_channel, ((0, 0), (0, MARGIN)))
    forward = forward_table()
    inverse = inverse_table()
    template_spec = jnp.dot(taps.reshape(-1, TL), forward[:TL], preferred_element_type=jnp.float32).astype(jnp.bfloat16)
    flat_channels = channels.reshape(-1).astype(jnp.int32)
    flat_shifts = shifts.reshape(-1).astype(jnp.int32)
    group = math.gcd(TEMPLATES, 64)
    count = TEMPLATES // group

    def one_window(window_index):
        tiles = lax.dynamic_slice_in_dim(padded, (window_index * WIN_DEV).astype(jnp.int32), NS, 1)
        spec = spectra(tiles, forward)

        def one_block(block_index):
            begin = (block_index * group * CH).astype(jnp.int32)
            spec_block = lax.dynamic_slice_in_dim(template_spec, begin, group * CH, 0)
            chan_block = lax.dynamic_slice_in_dim(flat_channels, begin, group * CH, 0)
            shift_block = lax.dynamic_slice_in_dim(flat_shifts, begin, group * CH, 0)
            data_spec = jnp.take(spec, chan_block, axis=0)
            return stack_block(spec_block, data_spec, shift_block, inverse)
        return lax.map(one_block, jnp.arange(count, dtype=jnp.int32)).reshape(TEMPLATES, WIN_DEV)
    stacks = lax.map(one_window, jnp.arange(N_WIN, dtype=jnp.int32))
    return jnp.transpose(stacks, (1, 0, 2)).reshape(TEMPLATES, TIMES)
```

```python
import functools
import math

import jax
import jax.numpy as jnp
import numpy as np
from jax import lax
from jax.experimental import pallas as pl
from jax.experimental.pallas import tpu as pltpu
from jax.sharding import PartitionSpec as P

WIN_DEV = 1024
TL = 400
CH = 30
DEC = 2
NTAP = 64
MOVE = 256
NS = 1792
NF = 896
LANE = 128
FB = NF // LANE
QB = 2 * FB
SLOT = 16
SPAN = DEC * LANE
MIB = 1 << 20


def cos_sin(rows, columns):
    angle = (np.arange(rows)[:, None] * np.arange(columns)[None, :] % NS) * (2.0 * math.pi / NS)
    return np.cos(angle), np.sin(angle)


def forward_table():
    c, s = cos_sin(NS, NF)
    return np.concatenate([c, s], axis=1).astype(jnp.bfloat16)


def inverse_table():
    c, s = cos_sin(NF, WIN_DEV)
    return np.concatenate([c, -s], axis=0).astype(jnp.bfloat16)


def phase_table():
    out = np.zeros((MOVE, 2, 8, LANE), np.float32)
    c, s = cos_sin(MOVE, NF)
    out[:, 0, :FB] = c.reshape(MOVE, FB, LANE)
    out[:, 1, :FB] = s.reshape(MOVE, FB, LANE)
    return out.reshape(MOVE, SLOT, LANE)


def weight_tile():
    w = np.full((NF,), 2.0 / (CH * NS), np.float32)
    w[0] = 1.0 / (CH * NS)
    out = np.zeros((8, LANE), np.float32)
    out[:FB] = w.reshape(FB, LANE)
    return out


def sub(q):
    return q if q < FB else q + 1


def front_kernel(raw_ref, fir_ref, table_ref, out_ref, seg, filt, tile):
    rows = raw_ref.shape[0]
    pieces = raw_ref.shape[1] // SPAN
    wins = out_ref.shape[0] // rows
    per = pieces // wins
    wide = jnp.broadcast_to(fir_ref[...], (LANE, 3 * LANE))
    band = pltpu.roll(wide, 0, 1, stride=DEC, stride_axis=0).astype(jnp.bfloat16)
    for b in range(pieces):
        here = pl.ds(b * rows, rows)
        seg[here, :SPAN] = raw_ref[:, b * SPAN:(b + 1) * SPAN]
        if b + 1 < pieces:
            seg[here, SPAN:] = raw_ref[:, (b + 1) * SPAN:(b + 1) * SPAN + LANE]
        else:
            seg[here, SPAN:] = jnp.zeros((rows, LANE), jnp.bfloat16)
    filt[pl.ds(0, pieces * rows), :] = lax.dot_general(
        seg[...], band, (((1,), (1,)), ((), ())), preferred_element_type=jnp.float32
    ).astype(jnp.bfloat16)
    filt[pl.ds(pieces * rows, FB * rows), :] = jnp.zeros((FB * rows, LANE), jnp.bfloat16)
    for w in range(wins):
        for q in range(QB):
            tile[pl.ds(w * rows, rows), q * LANE:(q + 1) * LANE] = filt[
                pl.ds((w * per + q) * rows, rows), :
            ]
    values = tile[...].astype(jnp.float32)
    scale = lax.rsqrt(jnp.mean(values * values, axis=1, keepdims=True) + 1e-05)
    out_ref[...] = (
        jnp.dot(tile[...], table_ref[...], preferred_element_type=jnp.float32) * scale
    ).astype(jnp.bfloat16)


def front(raw, fir, table, wins):
    rows, length = raw.shape
    pieces = length // SPAN
    wide = jnp.pad(fir.astype(jnp.float32).reshape(1, NTAP), ((0, 0), (0, 3 * LANE - NTAP)))
    return pl.pallas_call(
        front_kernel,
        out_shape=jax.ShapeDtypeStruct((wins * rows, NS), jnp.bfloat16),
        scratch_shapes=[
            pltpu.VMEM((pieces * rows, 3 * LANE), jnp.bfloat16),
            pltpu.VMEM(((pieces + FB) * rows, LANE), jnp.bfloat16),
            pltpu.VMEM((wins * rows, NS), jnp.bfloat16),
        ],
        compiler_params=pltpu.CompilerParams(vmem_limit_bytes=32 * MIB),
        name="front",
    )(raw, wide, table)


TB = 8
CP = 32


def template_kernel(shift_ref, taps_ref, head_ref, phase_ref, out_ref, lhs, spread):
    step = pl.program_id(0)
    for i in range(TB):
        lhs[pl.ds(i * CP, CH), :] = taps_ref[i]
    spec = jnp.dot(lhs[...], head_ref[...], preferred_element_type=jnp.float32)
    for q in range(QB):
        for g in range(TB * CP // 8):
            spread[pl.ds(g * 8 * SLOT + sub(q), 8, stride=SLOT), :] = spec[
                g * 8:(g + 1) * 8, q * LANE:(q + 1) * LANE
            ]

    def one(i, carry):
        for j in range(CH):
            base = pl.multiple_of((i * CP + j) * SLOT, SLOT)
            tc = spread[pl.ds(base, 8), :]
            ts = spread[pl.ds(pl.multiple_of(base + 8, 8), 8), :]
            s = shift_ref[step * TB + i, j]
            pc = phase_ref[s, 0:8, :]
            ps = phase_ref[s, 8:16, :]
            ur = tc * pc - ts * ps
            ui = ts * pc + tc * ps
            out_ref[i * CH + j] = jnp.concatenate([ur, ui], axis=0).astype(jnp.bfloat16)
        return carry

    lax.fori_loop(0, TB, one, 0)


def templates(taps, shifts, head, phase):
    count = taps.shape[0]
    return pl.pallas_call(
        template_kernel,
        out_shape=jax.ShapeDtypeStruct((count * CH, SLOT, LANE), jnp.bfloat16),
        grid_spec=pltpu.PrefetchScalarGridSpec(
            num_scalar_prefetch=1,
            grid=(count // TB,),
            in_specs=[
                pl.BlockSpec((TB, CH, TL), lambda i, s: (i, 0, 0)),
                pl.BlockSpec((TL, NS), lambda i, s: (0, 0)),
                pl.BlockSpec((MOVE, SLOT, LANE), lambda i, s: (0, 0, 0)),
            ],
            out_specs=pl.BlockSpec((TB * CH, SLOT, LANE), lambda i, s: (i, 0, 0)),
            scratch_shapes=[
                pltpu.VMEM((TB * CP, TL), jnp.bfloat16),
                pltpu.VMEM((TB * CP * SLOT, LANE), jnp.float32),
            ],
        ),
        compiler_params=pltpu.CompilerParams(vmem_limit_bytes=32 * MIB),
        cost_estimate=pl.CostEstimate(
            flops=2 * count * CH * TL * NS, bytes_accessed=30 * MIB, transcendentals=0
        ),
        name="templates",
    )(shifts, taps, head, phase)


KB = 8


def stack_kernel(row_ref, chan_ref, u_ref, x_ref, weight_ref, inverse_ref, out_ref, xs, z, packed):
    step = pl.program_id(0)

    @pl.when(step == 0)
    def _():
        def spread(i, carry):
            start = pl.multiple_of(i * 16, 16)
            for q in range(QB):
                v = x_ref[pl.ds(start, 16), q * LANE:(q + 1) * LANE].astype(jnp.float32)
                for h in range(2):
                    xs[pl.ds((start + 8 * h) * SLOT + sub(q), 8, stride=SLOT), :] = v[8 * h:8 * h + 8]
            return carry

        lax.fori_loop(0, x_ref.shape[0] // 16, spread, 0)

    def one(i, carry):
        zr = jnp.zeros((8, LANE), jnp.float32)
        zi = jnp.zeros((8, LANE), jnp.float32)
        for j in range(CH):
            row = row_ref[chan_ref[step * KB + i, j]]
            base = pl.multiple_of(row * SLOT, SLOT)
            xc = xs[pl.ds(base, 8), :]
            xn = xs[pl.ds(pl.multiple_of(base + 8, 8), 8), :]
            u = u_ref[i * CH + j].astype(jnp.float32)
            ur, ui = u[:8], u[8:]
            zr = zr + (ur * xc + ui * xn)
            zi = zi + (ui * xc - ur * xn)
        at = pl.multiple_of((step * KB + i) * SLOT, SLOT)
        z[pl.ds(at, 8), :] = zr * weight_ref[...]
        z[pl.ds(pl.multiple_of(at + 8, 8), 8), :] = zi * weight_ref[...]
        return carry

    lax.fori_loop(0, KB, one, 0)

    @pl.when(step == pl.num_programs(0) - 1)
    def _():
        count = packed.shape[0]
        for q in range(QB):
            for g in range(count // 16):
                halves = [
                    z[pl.ds((g * 16 + 8 * h) * SLOT + sub(q), 8, stride=SLOT), :] for h in range(2)
                ]
                packed[pl.ds(g * 16, 16), q * LANE:(q + 1) * LANE] = jnp.concatenate(
                    halves, axis=0
                ).astype(jnp.bfloat16)
        out_ref[...] = jnp.dot(packed[...], inverse_ref[...], preferred_element_type=jnp.float32)


def stacked(row_of, channels, u, x, weight, inverse):
    count = channels.shape[0]
    held = x.shape[0]
    one = pl.Buffered(1)
    return pl.pallas_call(
        stack_kernel,
        out_shape=jax.ShapeDtypeStruct((count, WIN_DEV), jnp.float32),
        grid_spec=pltpu.PrefetchScalarGridSpec(
            num_scalar_prefetch=2,
            grid=(count // KB,),
            in_specs=[
                pl.BlockSpec((KB * CH, SLOT, LANE), lambda i, r, c: (i, 0, 0)),
                pl.BlockSpec((held, NS), lambda i, r, c: (0, 0), pipeline_mode=one),
                pl.BlockSpec((8, LANE), lambda i, r, c: (0, 0)),
                pl.BlockSpec((NS, WIN_DEV), lambda i, r, c: (0, 0), pipeline_mode=one),
            ],
            out_specs=pl.BlockSpec((count, WIN_DEV), lambda i, r, c: (0, 0)),
            scratch_shapes=[
                pltpu.VMEM((held * SLOT, LANE), jnp.float32),
                pltpu.VMEM((count * SLOT, LANE), jnp.float32),
                pltpu.VMEM((count, NS), jnp.bfloat16),
            ],
        ),
        compiler_params=pltpu.CompilerParams(vmem_limit_bytes=56 * MIB),
        cost_estimate=pl.CostEstimate(
            flops=8 * count * CH * NF, bytes_accessed=30 * MIB, transcendentals=0
        ),
        name="stacked",
    )(row_of, channels, u, x, weight, inverse)


def on_device(raw, ids, fir, taps, channels, shifts):
    wins = lax.axis_size("win")
    tmpls = lax.axis_size("tmpl")
    slots = raw.shape[0]
    live_col = 3 * slots * wins // 5
    chan_total = live_col * tmpls
    held = -(-live_col // 16) * 16

    forward = forward_table()
    spec = front(raw, fir, jnp.asarray(forward), wins)
    mine = lax.all_to_all(
        spec.reshape(wins, slots, NS), "win", split_axis=0, concat_axis=0, tiled=True
    ).reshape(wins * slots, NS)

    grid = ids.reshape(wins, tmpls, slots).transpose(1, 0, 2).reshape(tmpls, wins * slots)
    live = grid >= 0
    rank = jnp.cumsum(live.astype(jnp.int32), axis=1) - 1
    place = jnp.arange(tmpls, dtype=jnp.int32)[:, None] * held + rank
    keyed = jnp.where(live, grid, chan_total)
    _, row_of = lax.sort((keyed.reshape(-1), place.reshape(-1)), num_keys=1)
    row_of = row_of[:chan_total]

    me = lax.axis_index("tmpl")
    my_rank = jnp.where(live, rank, -1)
    my_rank = lax.dynamic_slice_in_dim(my_rank, me, 1, 0)
    pick = (my_rank == jnp.arange(held, dtype=jnp.int32)[:, None]).astype(jnp.bfloat16)
    compact = jnp.dot(pick, mine, preferred_element_type=jnp.float32).astype(jnp.bfloat16)
    x = lax.all_gather(compact, "tmpl", axis=0, tiled=True)

    u = templates(taps, shifts, jnp.asarray(forward[:TL]), jnp.asarray(phase_table()))
    return stacked(
        row_of, channels, u, x, jnp.asarray(weight_tile()), jnp.asarray(inverse_table())
    )


def solution(mesh):
    return jax.shard_map(
        on_device,
        mesh=mesh,
        in_specs=(
            P(("win", "tmpl"), None),
            P(),
            P(),
            P("tmpl", None, None),
            P("tmpl", None),
            P("tmpl", None),
        ),
        out_specs=P("tmpl", "win"),
        check_vma=False,
    )
```

```python
import functools
import math

import jax
import jax.numpy as jnp
import numpy as np
from jax import lax
from jax.experimental import pallas as pl
from jax.experimental.pallas import tpu as pltpu
from jax.sharding import PartitionSpec as P

WIN_DEV = 1024
TL = 400
CH = 30
DEC = 2
NTAP = 64
MOVE = 256
NS = 1792
NF = 896
LANE = 128
FB = NF // LANE
QB = 2 * FB
SLOT = 16
SPAN = DEC * LANE
SLOTS = 16
TMPL = 16
MIB = 1 << 20


def cos_sin(rows, columns):
    angle = (np.arange(rows)[:, None] * np.arange(columns)[None, :] % NS) * (2.0 * math.pi / NS)
    return np.cos(angle), np.sin(angle)


def forward_table():
    c, s = cos_sin(NS, NF)
    return np.concatenate([c, s], axis=1).astype(jnp.bfloat16)


def inverse_table():
    c, s = cos_sin(NF, WIN_DEV)
    return np.concatenate([c, -s], axis=0).astype(jnp.bfloat16)


def phase_table():
    out = np.zeros((MOVE, 2, 8, LANE), np.float32)
    c, s = cos_sin(MOVE, NF)
    out[:, 0, :FB] = c.reshape(MOVE, FB, LANE)
    out[:, 1, :FB] = s.reshape(MOVE, FB, LANE)
    return out.reshape(MOVE, SLOT, LANE)


def weight_tile():
    w = np.full((NF,), 2.0 / (CH * NS), np.float32)
    w[0] = 1.0 / (CH * NS)
    out = np.zeros((8, LANE), np.float32)
    out[:FB] = w.reshape(FB, LANE)
    return out


def sub(q):
    return q if q < FB else q + 1


def dot(a, b, dims=((1,), (0,))):
    return lax.dot_general(a, b, (dims, ((), ())), preferred_element_type=jnp.float32)


def plan(ids_ref, rows_ref, rank_ref, held):
    ids = ids_ref[...]
    count, lanes = ids.shape
    group = lanes // SLOTS
    per = TMPL // group
    live = ids >= 0
    livef = live.astype(jnp.float32).astype(jnp.bfloat16)
    la = lax.broadcasted_iota(jnp.int32, (lanes, lanes), 0)
    lb = lax.broadcasted_iota(jnp.int32, (lanes, lanes), 1)
    same = (la // SLOTS) == (lb // SLOTS)
    total = dot(livef, same.astype(jnp.float32).astype(jnp.bfloat16)).astype(jnp.bfloat16)
    upto = dot(livef, (same & (la <= lb)).astype(jnp.float32).astype(jnp.bfloat16))
    ra = lax.broadcasted_iota(jnp.int32, (count, count), 0)
    rb = lax.broadcasted_iota(jnp.int32, (count, count), 1)
    before = ((ra % per) == (rb % per)) & (rb < ra)
    rank = upto + dot(before.astype(jnp.float32).astype(jnp.bfloat16), total)
    rank = jnp.where(live, rank, 0.0)
    row = lax.broadcasted_iota(jnp.int32, (count, lanes), 0)
    lane = lax.broadcasted_iota(jnp.int32, (count, lanes), 1)
    column = (row % per) * group + lane // SLOTS
    place = column * held + rank.astype(jnp.int32) - 1

    slots = count // per * SLOTS
    me = lax.axis_index("tmpl")
    sa = lax.broadcasted_iota(jnp.int32, (lanes, slots), 0)
    sb = lax.broadcasted_iota(jnp.int32, (lanes, slots), 1)
    chosen = sa == (me % group) * SLOTS + (sb % SLOTS)
    mine = dot(rank.astype(jnp.bfloat16), chosen.astype(jnp.float32).astype(jnp.bfloat16))
    oa = lax.broadcasted_iota(jnp.int32, (count, slots), 0)
    ob = lax.broadcasted_iota(jnp.int32, (count, slots), 1)
    mine = jnp.where(oa == (ob // SLOTS) * per + me // group, mine, 0.0)
    rank_ref[...] = jnp.broadcast_to(jnp.sum(mine, axis=0, keepdims=True), rank_ref.shape)

    high = rows_ref.shape[0]
    hi_iota = lax.broadcasted_iota(jnp.int32, (high, lanes), 0)
    lo_iota = lax.broadcasted_iota(jnp.int32, (LANE, lanes), 0)
    hi_sum = jnp.zeros((high, LANE), jnp.float32)
    lo_sum = jnp.zeros((high, LANE), jnp.float32)
    for r in range(count):
        label = ids[r:r + 1]
        at = place[r:r + 1]
        hit = hi_iota == (label >> 7)
        hi = jnp.where(hit, (at >> 6).astype(jnp.float32), 0.0).astype(jnp.bfloat16)
        lo = jnp.where(hit, (at & 63).astype(jnp.float32), 0.0).astype(jnp.bfloat16)
        low = (lo_iota == (label & 127)).astype(jnp.float32).astype(jnp.bfloat16)
        hi_sum = hi_sum + dot(hi, low, ((1,), (1,)))
        lo_sum = lo_sum + dot(lo, low, ((1,), (1,)))
    rows_ref[...] = hi_sum.astype(jnp.int32) * 64 + lo_sum.astype(jnp.int32)


def front_kernel(held, raw_ref, fir_ref, ids_ref, table_hbm, out_ref, rows_ref, rank_ref, seg, filt, tile, table, sem):
    fetch = pltpu.make_async_copy(table_hbm, table, sem)
    fetch.start()
    rows = raw_ref.shape[0]
    pieces = raw_ref.shape[1] // SPAN
    wins = out_ref.shape[0] // rows
    per = pieces // wins
    wide = jnp.broadcast_to(fir_ref[...], (LANE, 3 * LANE))
    band = pltpu.roll(wide, 0, 1, stride=DEC, stride_axis=0).astype(jnp.bfloat16)
    for b in range(pieces):
        here = pl.ds(b * rows, rows)
        seg[here, :SPAN] = raw_ref[:, b * SPAN:(b + 1) * SPAN]
        if b + 1 < pieces:
            seg[here, SPAN:] = raw_ref[:, (b + 1) * SPAN:(b + 1) * SPAN + LANE]
        else:
            seg[here, SPAN:] = jnp.zeros((rows, LANE), jnp.bfloat16)
    filt[pl.ds(0, pieces * rows), :] = dot(seg[...], band, ((1,), (1,))).astype(jnp.bfloat16)
    filt[pl.ds(pieces * rows, FB * rows), :] = jnp.zeros((FB * rows, LANE), jnp.bfloat16)
    for w in range(wins):
        for q in range(QB):
            tile[pl.ds(w * rows, rows), q * LANE:(q + 1) * LANE] = filt[
                pl.ds((w * per + q) * rows, rows), :
            ]
    plan(ids_ref, rows_ref, rank_ref, held)
    values = tile[...].astype(jnp.float32)
    scale = lax.rsqrt(jnp.mean(values * values, axis=1, keepdims=True) + 1e-05)
    fetch.wait()
    out_ref[...] = (dot(tile[...], table[...]) * scale).astype(jnp.bfloat16)


def front(raw, fir, ids, table, wins, held, high):
    rows, length = raw.shape
    pieces = length // SPAN
    wide = jnp.pad(fir.astype(jnp.float32).reshape(1, NTAP), ((0, 0), (0, 3 * LANE - NTAP)))
    vmem = pl.BlockSpec(memory_space=pltpu.VMEM)
    return pl.pallas_call(
        functools.partial(front_kernel, held),
        out_shape=(
            jax.ShapeDtypeStruct((wins * rows, NS), jnp.bfloat16),
            jax.ShapeDtypeStruct((high, LANE), jnp.int32),
            jax.ShapeDtypeStruct((8, wins * rows), jnp.float32),
        ),
        in_specs=[vmem, vmem, vmem, pl.BlockSpec(memory_space=pl.ANY)],
        out_specs=(vmem, vmem, vmem),
        scratch_shapes=[
            pltpu.VMEM((pieces * rows, 3 * LANE), jnp.bfloat16),
            pltpu.VMEM(((pieces + FB) * rows, LANE), jnp.bfloat16),
            pltpu.VMEM((wins * rows, NS), jnp.bfloat16),
            pltpu.VMEM((NS, NS), jnp.bfloat16),
            pltpu.SemaphoreType.DMA,
        ],
        compiler_params=pltpu.CompilerParams(vmem_limit_bytes=32 * MIB),
        name="front",
    )(raw, wide, ids, table)


JB = 2
UNROLL = 32


def template_spectra(shift_ref, taps, head, phase, u, spread):
    count = taps.shape[2]
    steps = taps.shape[0] // JB
    many = JB * count
    turns = count // UNROLL

    def one(step, carry):
        lhs = jnp.concatenate([taps[step * JB + j].T for j in range(JB)], axis=0)
        for c in range(NS // SPAN):
            spec = dot(lhs, head[:, c * SPAN:(c + 1) * SPAN])
            for h in range(2):
                for g in range(many // 8):
                    spread[pl.ds((g * QB + 2 * c + h) * 8, 8), :] = spec[
                        g * 8:(g + 1) * 8, h * LANE:(h + 1) * LANE
                    ]

        def rows(i, inner):
            for r in range(UNROLL):
                row = i * UNROLL + r
                base = i * (UNROLL // 8 * QB * 8) + (r // 8) * QB * 8 + r % 8
                tc = spread[pl.ds(base, 8, stride=8), :]
                ts = spread[pl.ds(base + FB * 8, 8, stride=8), :]
                s = shift_ref[step * JB + i // turns, (i % turns) * UNROLL + r]
                pc = phase[s, 0:8, :]
                ps = phase[s, 8:16, :]
                u[step * many + row] = jnp.concatenate(
                    [tc * pc - ts * ps, ts * pc + tc * ps], axis=0
                ).astype(jnp.bfloat16)
            return inner

        lax.fori_loop(0, many // UNROLL, rows, 0)
        return carry

    lax.fori_loop(0, steps, one, 0)


MESH = pl.DeviceIdType.MESH


def exchange_kernel(
    wins, rows_ref, chan_ref, shift_ref, spec_ref, rank_ref, weight_ref,
    taps_hbm, head_hbm, phase_hbm, inverse_hbm,
    out_ref,
    mine, wide, buf, u, spread, z, packed, taps, head, phase, inverse,
    fetch_sem, a_send, a_recv, g_send, g_recv,
):
    slots = spec_ref.shape[0] // wins
    w = lax.axis_index("win")
    t = lax.axis_index("tmpl")
    held = buf.shape[1]
    zl, x, c = t // 8, (t // 2) % 4, t % 2

    def ix(a, b, d):
        return (a * 4 + b) * 2 + d

    zo, xp, xm, x2, co = 1 - zl, lax.rem(x + 1, 4), lax.rem(x + 3, 4), lax.rem(x + 2, 4), 1 - c
    up, down, over, beside, me = ix(zl, xp, c), ix(zl, xm, c), ix(zo, x, c), ix(zl, x, co), ix(zl, x, c)

    barrier = pltpu.get_barrier_semaphore()
    for d in range(1, wins):
        pl.semaphore_signal(
            barrier, inc=1, device_id={"win": lax.rem(w + d, wins)}, device_id_type=MESH
        )
    for d in (up, down, over, beside):
        pl.semaphore_signal(barrier, inc=1, device_id={"tmpl": d}, device_id_type=MESH)

    fetches = [
        pltpu.make_async_copy(a, b, fetch_sem.at[i])
        for i, (a, b) in enumerate(
            ((taps_hbm, taps), (head_hbm, head), (phase_hbm, phase), (inverse_hbm, inverse))
        )
    ]
    for f in fetches:
        f.start()
    pl.semaphore_wait(barrier, wins + 3)

    def block(ref, i):
        return ref.at[pl.ds(pl.multiple_of(i * slots, slots), slots)]

    moves = []
    for d in range(1, wins):
        to = lax.rem(w + d, wins)
        move = pltpu.make_async_remote_copy(
            src_ref=block(spec_ref, to), dst_ref=block(mine, w),
            send_sem=a_send.at[d - 1], recv_sem=a_recv.at[d - 1],
            device_id={"win": to}, device_id_type=MESH,
        )
        move.start()
        moves.append(move)
    own = pl.ds(pl.multiple_of(w * slots, slots), slots)
    mine[own, :] = spec_ref[own, :]

    for f in fetches:
        f.wait()
    template_spectra(shift_ref, taps, head, phase, u, spread)

    for move in moves:
        move.wait_recv()
    tall = wide.shape[0] // SLOT
    order = lax.broadcasted_iota(jnp.int32, (tall, mine.shape[0]), 0).astype(jnp.float32) + 1.0
    pick = (order == rank_ref[0:1, :]).astype(jnp.float32).astype(jnp.bfloat16)
    for b in range(NS // SPAN):
        part = dot(pick, mine[:, b * SPAN:(b + 1) * SPAN])
        for h in range(2):
            for g in range(tall // 8):
                wide[pl.ds(g * 8 * SLOT + sub(2 * b + h), 8, stride=SLOT), :] = part[
                    g * 8:(g + 1) * 8, h * LANE:(h + 1) * LANE
                ]
    for g in range(held):
        buf[me, g] = wide[pl.ds(g * SLOT, SLOT), :].astype(jnp.bfloat16)

    cut = held * 2 // 5
    rest = held - cut
    low, high, whole = (0, cut), (cut, rest), (0, held)
    low1, low2 = (0, cut // 2), (cut // 2, cut - cut // 2)
    high1, high2 = (cut, rest // 2), (cut + rest // 2, rest - rest // 2)
    sends, beside_recv = [], []

    def copy(of, seg, to, k):
        ref = buf.at[of, pl.ds(seg[0], seg[1])]
        return pltpu.make_async_remote_copy(
            src_ref=ref, dst_ref=ref, send_sem=g_send.at[k], recv_sem=g_recv.at[k],
            device_id={"tmpl": to}, device_id_type=MESH,
        )

    def send(of, seg, to, back):
        k = len(sends)
        s = copy(of, seg, to, k)
        s.start()
        sends.append(s)
        return copy(back, seg, to, k)

    def relay(a, b, seg):
        beside_recv.append(send(ix(a, b, c), seg, beside, ix(a, b, co)))

    z_high = send(me, high, over, ix(zo, x, c))
    up_low = send(me, low, up, ix(zl, xm, c))
    down_low = send(me, low, down, ix(zl, xp, c))
    up_high = send(me, high, up, ix(zl, xm, c))
    down_high = send(me, high, down, ix(zl, xp, c))
    z_low = send(me, low, over, ix(zo, x, c))
    relay(zl, x, whole)
    up_low.wait_recv()
    up_low1 = send(ix(zl, xm, c), low1, up, ix(zl, x2, c))
    z_low_m = send(ix(zl, xm, c), low, over, ix(zo, xm, c))
    relay(zl, xm, low)
    down_low.wait_recv()
    down_low2 = send(ix(zl, xp, c), low2, down, ix(zl, x2, c))
    z_low_p = send(ix(zl, xp, c), low, over, ix(zo, xp, c))
    relay(zl, xp, low)
    z_high.wait_recv()
    up_z = send(ix(zo, x, c), high, up, ix(zo, xm, c))
    down_z = send(ix(zo, x, c), high, down, ix(zo, xp, c))
    relay(zo, x, high)
    up_high.wait_recv()
    up_high1 = send(ix(zl, xm, c), high1, up, ix(zl, x2, c))
    relay(zl, xm, high)
    down_high.wait_recv()
    down_high2 = send(ix(zl, xp, c), high2, down, ix(zl, x2, c))
    relay(zl, xp, high)
    z_low.wait_recv()
    relay(zo, x, low)
    up_low1.wait_recv()
    z_low1 = send(ix(zl, x2, c), low1, over, ix(zo, x2, c))
    relay(zl, x2, low1)
    down_low2.wait_recv()
    z_low2 = send(ix(zl, x2, c), low2, over, ix(zo, x2, c))
    relay(zl, x2, low2)
    up_z.wait_recv()
    up_z1 = send(ix(zo, xm, c), high1, up, ix(zo, x2, c))
    relay(zo, xm, high)
    down_z.wait_recv()
    down_z2 = send(ix(zo, xp, c), high2, down, ix(zo, x2, c))
    relay(zo, xp, high)
    z_low_m.wait_recv()
    relay(zo, xm, low)
    z_low_p.wait_recv()
    relay(zo, xp, low)
    up_high1.wait_recv()
    relay(zl, x2, high1)
    down_high2.wait_recv()
    relay(zl, x2, high2)
    z_low1.wait_recv()
    relay(zo, x2, low1)
    z_low2.wait_recv()
    relay(zo, x2, low2)
    up_z1.wait_recv()
    relay(zo, x2, high1)
    down_z2.wait_recv()
    relay(zo, x2, high2)
    for r in beside_recv:
        r.wait_recv()

    count = chan_ref.shape[1]
    flat = buf.reshape(buf.shape[0] * held, SLOT, LANE)

    def template(k):
        zr = [jnp.zeros((8, LANE), jnp.float32)] * 2
        zi = [jnp.zeros((8, LANE), jnp.float32)] * 2
        for j in range(CH):
            name = chan_ref[j, k]
            xv = flat[rows_ref[name >> 7, name & 127]].astype(jnp.float32)
            uv = u[j * count + k].astype(jnp.float32)
            xc, xs, ur, ui = xv[:8], xv[8:], uv[:8], uv[8:]
            a = j % 2
            zr[a] = zr[a] + (ur * xc + ui * xs)
            zi[a] = zi[a] + (ui * xc - ur * xs)
        at = pl.multiple_of(k * SLOT, SLOT)
        z[pl.ds(at, 8), :] = (zr[0] + zr[1]) * weight_ref[...]
        z[pl.ds(pl.multiple_of(at + 8, 8), 8), :] = (zi[0] + zi[1]) * weight_ref[...]

    def two(i, carry):
        template(2 * i)
        template(2 * i + 1)
        return carry

    lax.fori_loop(0, count // 2, two, 0)
    for q in range(QB):
        for g in range(count // 16):
            halves = [
                z[pl.ds((g * 16 + 8 * h) * SLOT + sub(q), 8, stride=SLOT), :] for h in range(2)
            ]
            packed[pl.ds(g * 16, 16), q * LANE:(q + 1) * LANE] = jnp.concatenate(
                halves, axis=0
            ).astype(jnp.bfloat16)
    out_ref[...] = dot(packed[...], inverse[...])

    for move in moves:
        move.wait_send()
    for s in sends:
        s.wait_send()


def exchange(rows, channels, shifts, spec, rank, taps, wins, tmpls, held):
    count = taps.shape[2]
    consts = (
        jnp.asarray(forward_table()[:TL]), jnp.asarray(phase_table()), jnp.asarray(inverse_table())
    )
    smem = pl.BlockSpec(memory_space=pltpu.SMEM)
    vmem = pl.BlockSpec(memory_space=pltpu.VMEM)
    hbm = pl.BlockSpec(memory_space=pl.ANY)
    tall = -(-held // 16) * 16
    return pl.pallas_call(
        functools.partial(exchange_kernel, wins),
        out_shape=jax.ShapeDtypeStruct((count, WIN_DEV), jnp.float32),
        in_specs=[smem, smem, smem, vmem, vmem, vmem, hbm, hbm, hbm, hbm],
        out_specs=vmem,
        scratch_shapes=[
            pltpu.VMEM(spec.shape, jnp.bfloat16),
            pltpu.VMEM((tall * SLOT, LANE), jnp.float32),
            pltpu.VMEM((tmpls, held, SLOT, LANE), jnp.bfloat16),
            pltpu.VMEM((count * CH, SLOT, LANE), jnp.bfloat16),
            pltpu.VMEM((JB * count * SLOT, LANE), jnp.float32),
            pltpu.VMEM((count * SLOT, LANE), jnp.float32),
            pltpu.VMEM((count, NS), jnp.bfloat16),
            pltpu.VMEM(taps.shape, jnp.bfloat16),
            pltpu.VMEM((TL, NS), jnp.bfloat16),
            pltpu.VMEM((MOVE, SLOT, LANE), jnp.float32),
            pltpu.VMEM((NS, WIN_DEV), jnp.bfloat16),
            pltpu.SemaphoreType.DMA((4,)),
            pltpu.SemaphoreType.DMA((wins - 1,)),
            pltpu.SemaphoreType.DMA((wins - 1,)),
            pltpu.SemaphoreType.DMA((37,)),
            pltpu.SemaphoreType.DMA((37,)),
        ],
        compiler_params=pltpu.CompilerParams(
            vmem_limit_bytes=58 * MIB, collective_id=0, has_side_effects=True
        ),
        name="exchange",
    )(rows, channels, shifts, spec, rank, jnp.asarray(weight_tile()), taps, *consts)


def on_device(raw, ids, fir, taps, channels, shifts):
    wins = lax.axis_size("win")
    tmpls = lax.axis_size("tmpl")
    held = 3 * SLOTS * wins // 5
    high = -(-held * tmpls // (8 * LANE)) * 8
    spec, rows, rank = front(
        raw, fir, ids.reshape(-1, LANE), jnp.asarray(forward_table()), wins, held, high
    )
    return exchange(
        rows, channels.T, shifts.T, spec, rank, jnp.transpose(taps, (1, 2, 0)), wins, tmpls, held
    )


def solution(mesh):
    return jax.shard_map(
        on_device,
        mesh=mesh,
        in_specs=(
            P(("win", "tmpl"), None),
            P(),
            P(),
            P("tmpl", None, None),
            P("tmpl", None),
            P("tmpl", None),
        ),
        out_specs=P("tmpl", "win"),
        check_vma=False,
    )
```

```python
import functools
import math

import jax
import jax.numpy as jnp
import numpy as np
from jax import lax
from jax.experimental import pallas as pl
from jax.experimental.pallas import tpu as pltpu
from jax.sharding import PartitionSpec as P

WIN_DEV = 1024
TL = 400
CH = 30
DEC = 2
NTAP = 64
MOVE = 256
NS = 1792
NF = 896
LANE = 128
FB = NF // LANE
QB = 2 * FB
SLOT = 16
SPAN = DEC * LANE
SLOTS = 16
TMPL = 16
CUT_C = 0
CUT_S = 61
MIB = 1 << 20


def cos_sin(rows, columns):
    angle = (np.arange(rows)[:, None] * np.arange(columns)[None, :] % NS) * (2.0 * math.pi / NS)
    return np.cos(angle), np.sin(angle)


def forward_table():
    c, s = cos_sin(NS, NF)
    return np.concatenate([c, s], axis=1).astype(jnp.bfloat16)


def inverse_table():
    c, s = cos_sin(NF, WIN_DEV)
    return np.concatenate([c, -s], axis=0).astype(jnp.bfloat16)


def phase_table():
    out = np.zeros((MOVE, 2, 8, LANE), np.float32)
    c, s = cos_sin(MOVE, NF)
    out[:, 0, :FB] = c.reshape(MOVE, FB, LANE)
    out[:, 1, :FB] = s.reshape(MOVE, FB, LANE)
    return out.reshape(MOVE, SLOT, LANE)


def weight_tile():
    w = np.full((NF,), 2.0 / (CH * NS), np.float32)
    w[0] = 1.0 / (CH * NS)
    out = np.zeros((8, LANE), np.float32)
    out[:FB] = w.reshape(FB, LANE)
    return out


def dot(a, b, dims=((1,), (0,))):
    return lax.dot_general(a, b, (dims, ((), ())), preferred_element_type=jnp.float32)


def plan(ids_ref, rows_ref, rank_ref, held):
    ids = ids_ref[...]
    count, lanes = ids.shape
    group = lanes // SLOTS
    per = TMPL // group
    live = ids >= 0
    livef = live.astype(jnp.float32).astype(jnp.bfloat16)
    la = lax.broadcasted_iota(jnp.int32, (lanes, lanes), 0)
    lb = lax.broadcasted_iota(jnp.int32, (lanes, lanes), 1)
    same = (la // SLOTS) == (lb // SLOTS)
    total = dot(livef, same.astype(jnp.float32).astype(jnp.bfloat16)).astype(jnp.bfloat16)
    upto = dot(livef, (same & (la <= lb)).astype(jnp.float32).astype(jnp.bfloat16))
    ra = lax.broadcasted_iota(jnp.int32, (count, count), 0)
    rb = lax.broadcasted_iota(jnp.int32, (count, count), 1)
    before = ((ra % per) == (rb % per)) & (rb < ra)
    rank = upto + dot(before.astype(jnp.float32).astype(jnp.bfloat16), total)
    rank = jnp.where(live, rank, 0.0)
    row = lax.broadcasted_iota(jnp.int32, (count, lanes), 0)
    lane = lax.broadcasted_iota(jnp.int32, (count, lanes), 1)
    column = (row % per) * group + lane // SLOTS
    place = column * held + rank.astype(jnp.int32) - 1

    slots = count // per * SLOTS
    me = lax.axis_index("tmpl")
    sa = lax.broadcasted_iota(jnp.int32, (lanes, slots), 0)
    sb = lax.broadcasted_iota(jnp.int32, (lanes, slots), 1)
    chosen = sa == (me % group) * SLOTS + (sb % SLOTS)
    mine = dot(rank.astype(jnp.bfloat16), chosen.astype(jnp.float32).astype(jnp.bfloat16))
    oa = lax.broadcasted_iota(jnp.int32, (count, slots), 0)
    ob = lax.broadcasted_iota(jnp.int32, (count, slots), 1)
    mine = jnp.where(oa == (ob // SLOTS) * per + me // group, mine, 0.0)
    rank_ref[...] = jnp.broadcast_to(jnp.sum(mine, axis=0, keepdims=True), rank_ref.shape)

    high = rows_ref.shape[0]
    hi_iota = lax.broadcasted_iota(jnp.int32, (high, lanes), 0)
    lo_iota = lax.broadcasted_iota(jnp.int32, (LANE, lanes), 0)
    hi_sum = jnp.zeros((high, LANE), jnp.float32)
    lo_sum = jnp.zeros((high, LANE), jnp.float32)
    for r in range(count):
        label = ids[r:r + 1]
        at = place[r:r + 1]
        hit = hi_iota == (label >> 7)
        hi = jnp.where(hit, (at >> 6).astype(jnp.float32), 0.0).astype(jnp.bfloat16)
        lo = jnp.where(hit, (at & 63).astype(jnp.float32), 0.0).astype(jnp.bfloat16)
        low = (lo_iota == (label & 127)).astype(jnp.float32).astype(jnp.bfloat16)
        hi_sum = hi_sum + dot(hi, low, ((1,), (1,)))
        lo_sum = lo_sum + dot(lo, low, ((1,), (1,)))
    found = hi_sum.astype(jnp.int32) * 64 + lo_sum.astype(jnp.int32)
    rows_ref[...] = jnp.clip(found, 0, TMPL * held - 1)


def sub(q):
    return q if q < FB else q + 1


JB = 2
UNROLL = 32
MESH = pl.DeviceIdType.MESH


def filtered_tiles(raw, fir, seg, filt, tile, taps_wide):
    rows = raw.shape[0]
    pieces = raw.shape[1] // SPAN
    wins = tile.shape[0] // rows
    per = pieces // wins
    taps_wide[...] = jnp.zeros_like(taps_wide)
    taps_wide[0:1, 0:NTAP] = fir[...].astype(jnp.float32)
    wide = jnp.broadcast_to(taps_wide[0:1, :], (LANE, 3 * LANE))
    band = pltpu.roll(wide, 0, 1, stride=DEC, stride_axis=0).astype(jnp.bfloat16)
    for b in range(pieces):
        here = pl.ds(b * rows, rows)
        seg[here, :SPAN] = raw[:, b * SPAN:(b + 1) * SPAN]
        if b + 1 < pieces:
            seg[here, SPAN:] = raw[:, (b + 1) * SPAN:(b + 1) * SPAN + LANE]
        else:
            seg[here, SPAN:] = jnp.zeros((rows, LANE), jnp.bfloat16)
    filt[pl.ds(0, pieces * rows), :] = dot(seg[...], band, ((1,), (1,))).astype(jnp.bfloat16)
    filt[pl.ds(pieces * rows, FB * rows), :] = jnp.zeros((FB * rows, LANE), jnp.bfloat16)
    for w in range(wins):
        for q in range(QB):
            tile[pl.ds(w * rows, rows), q * LANE:(q + 1) * LANE] = filt[
                pl.ds((w * per + q) * rows, rows), :
            ]
    values = tile[...].astype(jnp.float32)
    return lax.rsqrt(jnp.mean(values * values, axis=1, keepdims=True) + 1e-05)


def template_spectra(first, last, shift_ref, taps, head, phase, u, spread):
    count = taps.shape[2]
    many = JB * count
    turns = count // UNROLL

    def one(step, carry):
        lhs = jnp.concatenate([taps[step * JB + j].T for j in range(JB)], axis=0)
        for c in range(NS // SPAN):
            spec = dot(lhs, head[:, c * SPAN:(c + 1) * SPAN])
            for h in range(2):
                for g in range(many // 8):
                    spread[pl.ds((g * QB + 2 * c + h) * 8, 8), :] = spec[
                        g * 8:(g + 1) * 8, h * LANE:(h + 1) * LANE
                    ]

        def rows(i, inner):
            for r in range(UNROLL):
                row = i * UNROLL + r
                base = i * (UNROLL // 8 * QB * 8) + (r // 8) * QB * 8 + r % 8
                tc = spread[pl.ds(base, 8, stride=8), :]
                ts = spread[pl.ds(base + FB * 8, 8, stride=8), :]
                s = shift_ref[step * JB + i // turns, (i % turns) * UNROLL + r]
                pc = phase[s, 0:8, :]
                ps = phase[s, 8:16, :]
                u[step * many + row] = jnp.concatenate(
                    [tc * pc - ts * ps, ts * pc + tc * ps], axis=0
                ).astype(jnp.bfloat16)
            return inner

        lax.fori_loop(0, many // UNROLL, rows, 0)
        return carry

    lax.fori_loop(first, last, one, 0)


class Gather:
    def __init__(self, buf, cut, send_sem, recv_sem):
        t = lax.axis_index("tmpl")
        zl, x, c = t // 8, (t // 2) % 4, t % 2
        self.buf, self.ss, self.rs = buf, send_sem, recv_sem
        self.zl, self.x, self.zo = zl, x, 1 - zl
        self.xp, self.xm, self.x2 = lax.rem(x + 1, 4), lax.rem(x + 3, 4), lax.rem(x + 2, 4)
        self.ix = lambda a, b: (a * 4 + b) * 2 + c
        self.ox = lambda a, b: (a * 4 + b) * 2 + 1 - c
        self.up, self.down = self.ix(zl, self.xp), self.ix(zl, self.xm)
        self.over, self.beside = self.ix(self.zo, x), self.ox(zl, x)
        self.me = self.ix(zl, x)
        held = buf.shape[1]
        rest = held - cut
        self.low, self.high, self.whole = (0, cut), (cut, rest), (0, held)
        self.low1, self.low2 = (0, cut // 2), (cut // 2, cut - cut // 2)
        self.high1, self.high2 = (cut, rest // 2), (cut + rest // 2, rest - rest // 2)
        self.sends, self.last, self.wait = [], [], {}

    def copy(self, of, seg, to, k):
        ref = self.buf.at[of, pl.ds(seg[0], seg[1])]
        return pltpu.make_async_remote_copy(
            src_ref=ref, dst_ref=ref, send_sem=self.ss.at[k], recv_sem=self.rs.at[k],
            device_id={"tmpl": to}, device_id_type=MESH,
        )

    def send(self, name, of, seg, to, back):
        if seg[1]:
            k = len(self.sends)
            s = self.copy(of, seg, to, k)
            s.start()
            self.sends.append(s)
            self.wait[name] = self.copy(back, seg, to, k)

    def relay(self, a, b, seg):
        name = "beside" + str(len(self.last))
        self.send(name, self.ix(a, b), seg, self.beside, self.ox(a, b))
        if name in self.wait:
            self.last.append(self.wait[name])

    def came(self, name):
        if name in self.wait:
            self.wait[name].wait_recv()

    def start(self):
        ix, zl, zo, x, xm, xp = self.ix, self.zl, self.zo, self.x, self.xm, self.xp
        self.send("z high", self.me, self.high, self.over, ix(zo, x))
        self.send("up low", self.me, self.low, self.up, ix(zl, xm))
        self.send("down low", self.me, self.low, self.down, ix(zl, xp))
        self.send("up high", self.me, self.high, self.up, ix(zl, xm))
        self.send("down high", self.me, self.high, self.down, ix(zl, xp))
        self.send("z low", self.me, self.low, self.over, ix(zo, x))
        self.relay(zl, x, self.whole)

    def first(self):
        ix, zl, zo, x, xm, xp, x2 = self.ix, self.zl, self.zo, self.x, self.xm, self.xp, self.x2
        self.came("up low")
        self.send("up low1", ix(zl, xm), self.low1, self.up, ix(zl, x2))
        self.send("z low m", ix(zl, xm), self.low, self.over, ix(zo, xm))
        self.relay(zl, xm, self.low)
        self.came("down low")
        self.send("down low2", ix(zl, xp), self.low2, self.down, ix(zl, x2))
        self.send("z low p", ix(zl, xp), self.low, self.over, ix(zo, xp))
        self.relay(zl, xp, self.low)
        self.came("z high")
        self.send("up z", ix(zo, x), self.high, self.up, ix(zo, xm))
        self.send("down z", ix(zo, x), self.high, self.down, ix(zo, xp))
        self.relay(zo, x, self.high)

    def second(self):
        ix, zl, zo, x, xm, xp, x2 = self.ix, self.zl, self.zo, self.x, self.xm, self.xp, self.x2
        self.came("up high")
        self.send("up high1", ix(zl, xm), self.high1, self.up, ix(zl, x2))
        self.relay(zl, xm, self.high)
        self.came("down high")
        self.send("down high2", ix(zl, xp), self.high2, self.down, ix(zl, x2))
        self.relay(zl, xp, self.high)
        self.came("z low")
        self.relay(zo, x, self.low)

    def third(self):
        ix, zl, zo, xm, xp, x2 = self.ix, self.zl, self.zo, self.xm, self.xp, self.x2
        self.came("up low1")
        self.send("z low1", ix(zl, x2), self.low1, self.over, ix(zo, x2))
        self.relay(zl, x2, self.low1)
        self.came("down low2")
        self.send("z low2", ix(zl, x2), self.low2, self.over, ix(zo, x2))
        self.relay(zl, x2, self.low2)
        self.came("up z")
        self.send("up z1", ix(zo, xm), self.high1, self.up, ix(zo, x2))
        self.relay(zo, xm, self.high)
        self.came("down z")
        self.send("down z2", ix(zo, xp), self.high2, self.down, ix(zo, x2))
        self.relay(zo, xp, self.high)

    def fourth(self):
        for name, a, b, seg in (
            ("z low m", self.zo, self.xm, self.low), ("z low p", self.zo, self.xp, self.low),
            ("up high1", self.zl, self.x2, self.high1), ("down high2", self.zl, self.x2, self.high2),
        ):
            self.came(name)
            self.relay(a, b, seg)

    def finish(self):
        for name, a, b, seg in (
            ("z low1", self.zo, self.x2, self.low1), ("z low2", self.zo, self.x2, self.low2),
            ("up z1", self.zo, self.x2, self.high1), ("down z2", self.zo, self.x2, self.high2),
        ):
            self.came(name)
            self.relay(a, b, seg)
        for r in self.last:
            r.wait_recv()

    def drain(self):
        for s in self.sends:
            s.wait_send()


def match_kernel(
    wins,
    raw_hbm, fir_hbm, ids_hbm, chan_hbm, shift_hbm, taps_hbm, table_hbm, head_hbm, phase_hbm,
    weight_hbm, inverse_hbm,
    out_ref,
    raw, fir, ids, chan, shift, taps, table, head, phase, weight, inverse,
    fir_wide, seg, filt, tile, rank, rows_v, rows, spec, mine, wide, buf_c, buf_s, u, spread, z,
    packed, fetch_sem, a_send, a_recv, b_send, b_recv, c_send, c_recv, s_send, s_recv,
):
    slots = raw.shape[0]
    w = lax.axis_index("win")
    t = lax.axis_index("tmpl")
    held = buf_c.shape[1]
    moves_of = ((a_send, a_recv), (b_send, b_recv))
    bufs = (buf_c, buf_s)
    gathers = (
        Gather(buf_c, CUT_C, c_send, c_recv), Gather(buf_s, CUT_S, s_send, s_recv)
    )

    barrier = pltpu.get_barrier_semaphore()
    for d in range(1, wins):
        pl.semaphore_signal(
            barrier, inc=1, device_id={"win": lax.rem(w + d, wins)}, device_id_type=MESH
        )
    g = gathers[0]
    for d in (g.up, g.down, g.over, g.beside):
        pl.semaphore_signal(barrier, inc=1, device_id={"tmpl": d}, device_id_type=MESH)

    pairs = (
        (raw_hbm, raw), (fir_hbm, fir), (ids_hbm, ids), (table_hbm, table), (shift_hbm, shift),
        (chan_hbm, chan), (taps_hbm, taps), (head_hbm, head), (phase_hbm, phase),
        (weight_hbm, weight), (inverse_hbm, inverse),
    )
    fetches = [
        pltpu.make_async_copy(a, b, fetch_sem.at[i]) for i, (a, b) in enumerate(pairs)
    ]
    for f in fetches:
        f.start()

    fetches[0].wait()
    fetches[1].wait()
    scale = filtered_tiles(raw, fir, seg, filt, tile, fir_wide)
    fetches[3].wait()

    def block(ref, half, i):
        return ref.at[half, pl.ds(pl.multiple_of(i * slots, slots), slots)]

    own = pl.ds(pl.multiple_of(w * slots, slots), slots)
    moves = ([], [])
    for half in range(2):
        spec[half] = (dot(tile[...], table[:, half * NF:(half + 1) * NF]) * scale).astype(
            jnp.bfloat16
        )
        if half == 0:
            pl.semaphore_wait(barrier, wins + 3)
        for d in range(1, wins):
            to = lax.rem(w + d, wins)
            move = pltpu.make_async_remote_copy(
                src_ref=block(spec, half, to), dst_ref=block(mine, half, w),
                send_sem=moves_of[half][0].at[d - 1], recv_sem=moves_of[half][1].at[d - 1],
                device_id={"win": to}, device_id_type=MESH,
            )
            move.start()
            moves[half].append(move)
        mine[half, own, :] = spec[half, own, :]

    fetches[2].wait()
    plan(ids, rows_v, rank, held)
    table_out = pltpu.make_async_copy(rows_v, rows, fetch_sem.at[len(pairs)])
    table_out.start()
    for f in fetches[4:9]:
        f.wait()

    def templates(first, last):
        template_spectra(first, last, shift, taps, head, phase, u, spread)

    tall = wide.shape[0] // 8

    def compact(half):
        for move in moves[half]:
            move.wait_recv()
        order = lax.broadcasted_iota(jnp.int32, (tall, mine.shape[1]), 0).astype(jnp.float32) + 1.0
        pick = (order == rank[0:1, :]).astype(jnp.float32).astype(jnp.bfloat16)
        part = dot(pick, mine[half])
        for q in range(FB):
            for i in range(tall // 8):
                wide[pl.ds(i * 64 + q, 8, stride=8), :] = part[
                    i * 8:(i + 1) * 8, q * LANE:(q + 1) * LANE
                ]
        for i in range(held):
            bufs[half][t, i] = wide[pl.ds(i * 8, 8), :].astype(jnp.bfloat16)

    count = chan.shape[1]
    flats = [b.reshape(b.shape[0] * held, 8, LANE) for b in bufs]

    def template(half, k):
        zr = [jnp.zeros((8, LANE), jnp.float32)] * 2
        zi = [jnp.zeros((8, LANE), jnp.float32)] * 2
        for j in range(CH):
            name = chan[j, k]
            xv = flats[half][rows[name >> 7, name & 127]].astype(jnp.float32)
            uv = u[j * count + k].astype(jnp.float32)
            ur, ui = uv[:8], uv[8:]
            a = j % 2
            if half == 0:
                zr[a] = zr[a] + ur * xv
                zi[a] = zi[a] + ui * xv
            else:
                zr[a] = zr[a] + ui * xv
                zi[a] = zi[a] - ur * xv
        at = pl.ds(pl.multiple_of(k * SLOT, SLOT), 8)
        more = pl.ds(pl.multiple_of(k * SLOT + 8, 8), 8)
        if half == 0:
            z[at, :] = zr[0] + zr[1]
            z[more, :] = zi[0] + zi[1]
        else:
            z[at, :] = (z[at, :] + (zr[0] + zr[1])) * weight[...]
            z[more, :] = (z[more, :] + (zi[0] + zi[1])) * weight[...]

    def stack(half, first, last):
        def two(i, carry):
            template(half, 2 * i)
            template(half, 2 * i + 1)
            return carry

        lax.fori_loop(first // 2, last // 2, two, 0)

    c, s = gathers
    q4 = count // 4
    templates(0, 5)
    table_out.wait()
    compact(0)
    c.start()
    templates(5, 7)
    c.first()
    templates(7, 8)
    c.second()
    templates(8, 10)
    compact(1)
    s.start()
    templates(10, 12)
    c.third()
    templates(12, 13)
    s.first()
    c.fourth()
    templates(13, 15)
    s.second()
    c.finish()
    for f in fetches[9:]:
        f.wait()
    stack(0, 0, q4)
    s.third()
    stack(0, q4, 2 * q4)
    s.fourth()
    stack(0, 2 * q4, 4 * q4)
    s.finish()
    stack(1, 0, count)
    for q in range(QB):
        for i in range(count // 16):
            halves = [
                z[pl.ds((i * 16 + 8 * h) * SLOT + sub(q), 8, stride=SLOT), :] for h in range(2)
            ]
            packed[pl.ds(i * 16, 16), q * LANE:(q + 1) * LANE] = jnp.concatenate(
                halves, axis=0
            ).astype(jnp.bfloat16)
    out_ref[...] = dot(packed[...], inverse[...])

    for half in range(2):
        for move in moves[half]:
            move.wait_send()
        gathers[half].drain()


def matched(raw, fir, ids, channels, shifts, taps, wins, tmpls, held):
    count = taps.shape[2]
    slots, length = raw.shape
    pieces = length // SPAN
    high = -(-held * tmpls // (8 * LANE)) * 8
    tall = -(-held // 16) * 16
    forward = forward_table()
    args = (
        raw, fir.reshape(1, -1), ids.reshape(-1, LANE), channels, shifts, taps,
        jnp.asarray(forward), jnp.asarray(forward[:TL]), jnp.asarray(phase_table()),
        jnp.asarray(weight_tile()), jnp.asarray(inverse_table()),
    )
    smem = (3, 4)
    staged = [
        (pltpu.SMEM if i in smem else pltpu.VMEM)(a.shape, a.dtype) for i, a in enumerate(args)
    ]
    dma = pltpu.SemaphoreType.DMA
    return pl.pallas_call(
        functools.partial(match_kernel, wins),
        out_shape=jax.ShapeDtypeStruct((count, WIN_DEV), jnp.float32),
        in_specs=[pl.BlockSpec(memory_space=pl.ANY)] * len(args),
        out_specs=pl.BlockSpec(memory_space=pltpu.VMEM),
        scratch_shapes=staged + [
            pltpu.VMEM((8, 3 * LANE), jnp.float32),
            pltpu.VMEM((pieces * slots, 3 * LANE), jnp.bfloat16),
            pltpu.VMEM(((pieces + FB) * slots, LANE), jnp.bfloat16),
            pltpu.VMEM((wins * slots, NS), jnp.bfloat16),
            pltpu.VMEM((8, wins * slots), jnp.float32),
            pltpu.VMEM((high, LANE), jnp.int32),
            pltpu.SMEM((high, LANE), jnp.int32),
            pltpu.VMEM((2, wins * slots, NF), jnp.bfloat16),
            pltpu.VMEM((2, wins * slots, NF), jnp.bfloat16),
            pltpu.VMEM((tall * 8, LANE), jnp.float32),
            pltpu.VMEM((tmpls, held, 8, LANE), jnp.bfloat16),
            pltpu.VMEM((tmpls, held, 8, LANE), jnp.bfloat16),
            pltpu.VMEM((count * CH, SLOT, LANE), jnp.bfloat16),
            pltpu.VMEM((JB * count * SLOT, LANE), jnp.float32),
            pltpu.VMEM((count * SLOT, LANE), jnp.float32),
            pltpu.VMEM((count, NS), jnp.bfloat16),
            dma((len(args) + 1,)),
            dma((wins - 1,)), dma((wins - 1,)), dma((wins - 1,)), dma((wins - 1,)),
            dma((37,)), dma((37,)), dma((37,)), dma((37,)),
        ],
        compiler_params=pltpu.CompilerParams(
            vmem_limit_bytes=62 * MIB, collective_id=0, has_side_effects=True
        ),
        name="matched",
    )(*args)


def on_device(raw, ids, fir, taps, channels, shifts):
    wins = lax.axis_size("win")
    tmpls = lax.axis_size("tmpl")
    held = 3 * SLOTS * wins // 5
    return matched(
        raw, fir, ids, channels.T, shifts.T, jnp.transpose(taps, (1, 2, 0)), wins, tmpls, held
    )


def solution(mesh):
    return jax.shard_map(
        on_device,
        mesh=mesh,
        in_specs=(
            P(("win", "tmpl"), None),
            P(),
            P(),
            P("tmpl", None, None),
            P("tmpl", None),
            P("tmpl", None),
        ),
        out_specs=P("tmpl", "win"),
        check_vma=False,
    )
```

```python
import functools
import math

import jax
import jax.numpy as jnp
import numpy as np
from jax import lax
from jax.experimental import pallas as pl
from jax.experimental.pallas import tpu as pltpu
from jax.sharding import PartitionSpec as P

WIN_DEV = 1024
TL = 400
CH = 30
DEC = 2
NTAP = 64
MOVE = 256
NS = 1792
NF = 896
LANE = 128
FB = NF // LANE
QB = 2 * FB
SLOT = 16
SPAN = DEC * LANE
SLOTS = 16
TMPL = 16
CUT_C = 61
CUT_S = 61
MIB = 1 << 20


def cos_sin(rows, columns):
    angle = (np.arange(rows)[:, None] * np.arange(columns)[None, :] % NS) * (2.0 * math.pi / NS)
    return np.cos(angle), np.sin(angle)


def forward_table():
    c, s = cos_sin(NS, NF)
    return np.concatenate([c, s], axis=1).astype(jnp.bfloat16)


def inverse_table():
    c, s = cos_sin(NF, WIN_DEV)
    return np.concatenate([c, -s], axis=0).astype(jnp.bfloat16)


def phase_table():
    out = np.zeros((MOVE, 2, 8, LANE), np.float32)
    c, s = cos_sin(MOVE, NF)
    out[:, 0, :FB] = c.reshape(MOVE, FB, LANE)
    out[:, 1, :FB] = s.reshape(MOVE, FB, LANE)
    return out.reshape(MOVE, SLOT, LANE)


def weight_tile():
    w = np.full((NF,), 2.0 / (CH * NS), np.float32)
    w[0] = 1.0 / (CH * NS)
    out = np.zeros((8, LANE), np.float32)
    out[:FB] = w.reshape(FB, LANE)
    return out


def dot(a, b, dims=((1,), (0,))):
    return lax.dot_general(a, b, (dims, ((), ())), preferred_element_type=jnp.float32)


def plan(ids_ref, chan_ref, index_ref, rank_ref, held, high):
    ids = ids_ref[...]
    count, lanes = ids.shape
    group = lanes // SLOTS
    per = TMPL // group
    live = ids >= 0
    livef = live.astype(jnp.float32).astype(jnp.bfloat16)
    la = lax.broadcasted_iota(jnp.int32, (lanes, lanes), 0)
    lb = lax.broadcasted_iota(jnp.int32, (lanes, lanes), 1)
    same = (la // SLOTS) == (lb // SLOTS)
    total = dot(livef, same.astype(jnp.float32).astype(jnp.bfloat16)).astype(jnp.bfloat16)
    upto = dot(livef, (same & (la <= lb)).astype(jnp.float32).astype(jnp.bfloat16))
    ra = lax.broadcasted_iota(jnp.int32, (count, count), 0)
    rb = lax.broadcasted_iota(jnp.int32, (count, count), 1)
    before = ((ra % per) == (rb % per)) & (rb < ra)
    rank = upto + dot(before.astype(jnp.float32).astype(jnp.bfloat16), total)
    rank = jnp.where(live, rank, 0.0)
    row = lax.broadcasted_iota(jnp.int32, (count, lanes), 0)
    lane = lax.broadcasted_iota(jnp.int32, (count, lanes), 1)
    column = (row % per) * group + lane // SLOTS
    place = column * held + rank.astype(jnp.int32) - 1

    slots = count // per * SLOTS
    me = lax.axis_index("tmpl")
    sa = lax.broadcasted_iota(jnp.int32, (lanes, slots), 0)
    sb = lax.broadcasted_iota(jnp.int32, (lanes, slots), 1)
    chosen = sa == (me % group) * SLOTS + (sb % SLOTS)
    mine = dot(rank.astype(jnp.bfloat16), chosen.astype(jnp.float32).astype(jnp.bfloat16))
    oa = lax.broadcasted_iota(jnp.int32, (count, slots), 0)
    ob = lax.broadcasted_iota(jnp.int32, (count, slots), 1)
    mine = jnp.where(oa == (ob // SLOTS) * per + me // group, mine, 0.0)
    rank_ref[...] = jnp.broadcast_to(jnp.sum(mine, axis=0, keepdims=True), rank_ref.shape)

    hi_iota = lax.broadcasted_iota(jnp.int32, (high, lanes), 0)
    lo_iota = lax.broadcasted_iota(jnp.int32, (LANE, lanes), 0)
    hi_sum = jnp.zeros((high, LANE), jnp.float32)
    lo_sum = jnp.zeros((high, LANE), jnp.float32)
    for r in range(count):
        label = ids[r:r + 1]
        at = place[r:r + 1]
        hit = hi_iota == (label >> 7)
        hi = jnp.where(hit, (at >> 6).astype(jnp.float32), 0.0).astype(jnp.bfloat16)
        lo = jnp.where(hit, (at & 63).astype(jnp.float32), 0.0).astype(jnp.bfloat16)
        low = (lo_iota == (label & 127)).astype(jnp.float32).astype(jnp.bfloat16)
        hi_sum = hi_sum + dot(hi, low, ((1,), (1,)))
        lo_sum = lo_sum + dot(lo, low, ((1,), (1,)))
    both = jnp.concatenate([hi_sum, lo_sum], axis=0).astype(jnp.bfloat16)
    for j in range(chan_ref.shape[0]):
        name = chan_ref[j:j + 1, :]
        low = (lo_iota == (name & 127)).astype(jnp.float32).astype(jnp.bfloat16)
        got = dot(both, low)
        hit = hi_iota == (name >> 7)
        hi = jnp.sum(jnp.where(hit, got[:high], 0.0), axis=0, keepdims=True)
        lo = jnp.sum(jnp.where(hit, got[high:], 0.0), axis=0, keepdims=True)
        found = hi.astype(jnp.int32) * 64 + lo.astype(jnp.int32)
        index_ref[j:j + 1, :] = jnp.clip(found, 0, TMPL * held - 1)


def sub(q):
    return q if q < FB else q + 1


JB = 2
UNROLL = 32
MESH = pl.DeviceIdType.MESH


def filtered_tiles(raw, fir, seg, filt, tile, taps_wide):
    rows = raw.shape[0]
    pieces = raw.shape[1] // SPAN
    wins = tile.shape[0] // rows
    per = pieces // wins
    taps_wide[...] = jnp.zeros_like(taps_wide)
    taps_wide[0:1, 0:NTAP] = fir[...].astype(jnp.float32)
    wide = jnp.broadcast_to(taps_wide[0:1, :], (LANE, 3 * LANE))
    band = pltpu.roll(wide, 0, 1, stride=DEC, stride_axis=0).astype(jnp.bfloat16)
    for b in range(pieces):
        here = pl.ds(b * rows, rows)
        seg[here, :SPAN] = raw[:, b * SPAN:(b + 1) * SPAN]
        if b + 1 < pieces:
            seg[here, SPAN:] = raw[:, (b + 1) * SPAN:(b + 1) * SPAN + LANE]
        else:
            seg[here, SPAN:] = jnp.zeros((rows, LANE), jnp.bfloat16)
    filt[pl.ds(0, pieces * rows), :] = dot(seg[...], band, ((1,), (1,))).astype(jnp.bfloat16)
    filt[pl.ds(pieces * rows, FB * rows), :] = jnp.zeros((FB * rows, LANE), jnp.bfloat16)
    for w in range(wins):
        for q in range(QB):
            tile[pl.ds(w * rows, rows), q * LANE:(q + 1) * LANE] = filt[
                pl.ds((w * per + q) * rows, rows), :
            ]
    values = tile[...].astype(jnp.float32)
    return lax.rsqrt(jnp.mean(values * values, axis=1, keepdims=True) + 1e-05)


def template_spectra(first, last, shift_ref, taps, head, phase, u, spread):
    count = taps.shape[2]
    many = JB * count
    turns = count // UNROLL

    def one(step, carry):
        lhs = jnp.concatenate([taps[step * JB + j].T for j in range(JB)], axis=0)
        for c in range(NS // SPAN):
            spec = dot(lhs, head[:, c * SPAN:(c + 1) * SPAN])
            for h in range(2):
                for g in range(many // 8):
                    spread[pl.ds((g * QB + 2 * c + h) * 8, 8), :] = spec[
                        g * 8:(g + 1) * 8, h * LANE:(h + 1) * LANE
                    ]

        def rows(i, inner):
            for r in range(UNROLL):
                row = i * UNROLL + r
                base = i * (UNROLL // 8 * QB * 8) + (r // 8) * QB * 8 + r % 8
                tc = spread[pl.ds(base, 8, stride=8), :]
                ts = spread[pl.ds(base + FB * 8, 8, stride=8), :]
                s = shift_ref[step * JB + i // turns, (i % turns) * UNROLL + r]
                pc = phase[s, 0:8, :]
                ps = phase[s, 8:16, :]
                u[step * many + row] = jnp.concatenate(
                    [tc * pc - ts * ps, ts * pc + tc * ps], axis=0
                ).astype(jnp.bfloat16)
            return inner

        lax.fori_loop(0, many // UNROLL, rows, 0)
        return carry

    lax.fori_loop(first, last, one, 0)


class Gather:
    def __init__(self, buf, cut, send_sem, recv_sem):
        t = lax.axis_index("tmpl")
        zl, x, c = t // 8, (t // 2) % 4, t % 2
        self.buf, self.ss, self.rs = buf, send_sem, recv_sem
        self.zl, self.x, self.zo = zl, x, 1 - zl
        self.xp, self.xm, self.x2 = lax.rem(x + 1, 4), lax.rem(x + 3, 4), lax.rem(x + 2, 4)
        self.ix = lambda a, b: (a * 4 + b) * 2 + c
        self.ox = lambda a, b: (a * 4 + b) * 2 + 1 - c
        self.up, self.down = self.ix(zl, self.xp), self.ix(zl, self.xm)
        self.over, self.beside = self.ix(self.zo, x), self.ox(zl, x)
        self.me = self.ix(zl, x)
        held = buf.shape[1]
        rest = held - cut
        self.low, self.high, self.whole = (0, cut), (cut, rest), (0, held)
        self.low1, self.low2 = (0, cut // 2), (cut // 2, cut - cut // 2)
        self.high1, self.high2 = (cut, rest // 2), (cut + rest // 2, rest - rest // 2)
        self.sends, self.last, self.wait = [], [], {}

    def copy(self, of, seg, to, k):
        ref = self.buf.at[of, pl.ds(seg[0], seg[1])]
        return pltpu.make_async_remote_copy(
            src_ref=ref, dst_ref=ref, send_sem=self.ss.at[k], recv_sem=self.rs.at[k],
            device_id={"tmpl": to}, device_id_type=MESH,
        )

    def send(self, name, of, seg, to, back):
        if seg[1]:
            k = len(self.sends)
            s = self.copy(of, seg, to, k)
            s.start()
            self.sends.append(s)
            self.wait[name] = self.copy(back, seg, to, k)

    def relay(self, a, b, seg):
        name = "beside" + str(len(self.last))
        self.send(name, self.ix(a, b), seg, self.beside, self.ox(a, b))
        if name in self.wait:
            self.last.append(self.wait[name])

    def came(self, name):
        if name in self.wait:
            self.wait[name].wait_recv()

    def start(self):
        ix, zl, zo, x, xm, xp = self.ix, self.zl, self.zo, self.x, self.xm, self.xp
        self.send("z high", self.me, self.high, self.over, ix(zo, x))
        self.send("up low", self.me, self.low, self.up, ix(zl, xm))
        self.send("down low", self.me, self.low, self.down, ix(zl, xp))
        self.send("up high", self.me, self.high, self.up, ix(zl, xm))
        self.send("down high", self.me, self.high, self.down, ix(zl, xp))
        self.send("z low", self.me, self.low, self.over, ix(zo, x))
        self.relay(zl, x, self.whole)

    def first(self):
        ix, zl, zo, x, xm, xp, x2 = self.ix, self.zl, self.zo, self.x, self.xm, self.xp, self.x2
        self.came("up low")
        self.send("up low1", ix(zl, xm), self.low1, self.up, ix(zl, x2))
        self.send("z low m", ix(zl, xm), self.low, self.over, ix(zo, xm))
        self.relay(zl, xm, self.low)
        self.came("down low")
        self.send("down low2", ix(zl, xp), self.low2, self.down, ix(zl, x2))
        self.send("z low p", ix(zl, xp), self.low, self.over, ix(zo, xp))
        self.relay(zl, xp, self.low)
        self.came("z high")
        self.send("up z", ix(zo, x), self.high, self.up, ix(zo, xm))
        self.send("down z", ix(zo, x), self.high, self.down, ix(zo, xp))
        self.relay(zo, x, self.high)

    def second(self):
        ix, zl, zo, x, xm, xp, x2 = self.ix, self.zl, self.zo, self.x, self.xm, self.xp, self.x2
        self.came("up high")
        self.send("up high1", ix(zl, xm), self.high1, self.up, ix(zl, x2))
        self.relay(zl, xm, self.high)
        self.came("down high")
        self.send("down high2", ix(zl, xp), self.high2, self.down, ix(zl, x2))
        self.relay(zl, xp, self.high)
        self.came("z low")
        self.relay(zo, x, self.low)

    def third(self):
        ix, zl, zo, xm, xp, x2 = self.ix, self.zl, self.zo, self.xm, self.xp, self.x2
        self.came("up low1")
        self.send("z low1", ix(zl, x2), self.low1, self.over, ix(zo, x2))
        self.relay(zl, x2, self.low1)
        self.came("down low2")
        self.send("z low2", ix(zl, x2), self.low2, self.over, ix(zo, x2))
        self.relay(zl, x2, self.low2)
        self.came("up z")
        self.send("up z1", ix(zo, xm), self.high1, self.up, ix(zo, x2))
        self.relay(zo, xm, self.high)
        self.came("down z")
        self.send("down z2", ix(zo, xp), self.high2, self.down, ix(zo, x2))
        self.relay(zo, xp, self.high)

    def fourth(self):
        for name, a, b, seg in (
            ("z low m", self.zo, self.xm, self.low), ("z low p", self.zo, self.xp, self.low),
            ("up high1", self.zl, self.x2, self.high1), ("down high2", self.zl, self.x2, self.high2),
        ):
            self.came(name)
            self.relay(a, b, seg)

    def finish(self):
        for name, a, b, seg in (
            ("z low1", self.zo, self.x2, self.low1), ("z low2", self.zo, self.x2, self.low2),
            ("up z1", self.zo, self.x2, self.high1), ("down z2", self.zo, self.x2, self.high2),
        ):
            self.came(name)
            self.relay(a, b, seg)
        for r in self.last:
            r.wait_recv()

    def drain(self):
        for s in self.sends:
            s.wait_send()


def match_kernel(
    wins,
    raw_hbm, fir_hbm, ids_hbm, chan_hbm, shift_hbm, taps_hbm, table_hbm, head_hbm, phase_hbm,
    weight_hbm, inverse_hbm,
    out_ref,
    raw, fir, ids, chan, shift, taps, table, head, phase, weight, inverse,
    fir_wide, seg, filt, tile, rank, index_v, index, spec, mine, wide, buf_c, buf_s, u, spread, z,
    packed, fetch_sem, a_send, a_recv, b_send, b_recv, c_send, c_recv, s_send, s_recv,
):
    slots = raw.shape[0]
    w = lax.axis_index("win")
    t = lax.axis_index("tmpl")
    held = buf_c.shape[1]
    moves_of = ((a_send, a_recv), (b_send, b_recv))
    bufs = (buf_c, buf_s)
    gathers = (
        Gather(buf_c, CUT_C, c_send, c_recv), Gather(buf_s, CUT_S, s_send, s_recv)
    )

    barrier = pltpu.get_barrier_semaphore()
    for d in range(1, wins):
        pl.semaphore_signal(
            barrier, inc=1, device_id={"win": lax.rem(w + d, wins)}, device_id_type=MESH
        )
    g = gathers[0]
    for d in (g.up, g.down, g.over, g.beside):
        pl.semaphore_signal(barrier, inc=1, device_id={"tmpl": d}, device_id_type=MESH)

    pairs = (
        (raw_hbm, raw), (fir_hbm, fir), (table_hbm.at[0], table.at[0]),
        (table_hbm.at[1], table.at[1]), (ids_hbm, ids), (chan_hbm, chan), (shift_hbm, shift),
        (taps_hbm, taps), (head_hbm, head), (phase_hbm, phase),
        (weight_hbm, weight), (inverse_hbm, inverse),
    )
    fetches = [
        pltpu.make_async_copy(a, b, fetch_sem.at[i]) for i, (a, b) in enumerate(pairs)
    ]
    for f in fetches[:7]:
        f.start()

    fetches[0].wait()
    fetches[1].wait()
    scale = filtered_tiles(raw, fir, seg, filt, tile, fir_wide)

    def block(ref, half, i):
        return ref.at[half, pl.ds(pl.multiple_of(i * slots, slots), slots)]

    own = pl.ds(pl.multiple_of(w * slots, slots), slots)
    moves = ([], [])
    for half in range(2):
        fetches[2 + half].wait()
        spec[half] = (dot(tile[...], table[half]) * scale).astype(
            jnp.bfloat16
        )
        if half == 0:
            pl.semaphore_wait(barrier, wins + 3)
        for d in range(1, wins):
            to = lax.rem(w + d, wins)
            move = pltpu.make_async_remote_copy(
                src_ref=block(spec, half, to), dst_ref=block(mine, half, w),
                send_sem=moves_of[half][0].at[d - 1], recv_sem=moves_of[half][1].at[d - 1],
                device_id={"win": to}, device_id_type=MESH,
            )
            move.start()
            moves[half].append(move)
        mine[half, own, :] = spec[half, own, :]

    for f in fetches[7:]:
        f.start()
    fetches[4].wait()
    fetches[5].wait()
    plan(ids, chan, index_v, rank, held, -(-held * TMPL // (8 * LANE)) * 8)
    table_out = pltpu.make_async_copy(index_v, index, fetch_sem.at[len(pairs)])
    table_out.start()
    for f in fetches[6:10]:
        f.wait()

    def templates(first, last):
        template_spectra(first, last, shift, taps, head, phase, u, spread)

    tall = wide.shape[0] // 8

    def compact(half):
        for move in moves[half]:
            move.wait_recv()
        order = lax.broadcasted_iota(jnp.int32, (tall, mine.shape[1]), 0).astype(jnp.float32) + 1.0
        pick = (order == rank[0:1, :]).astype(jnp.float32).astype(jnp.bfloat16)
        part = dot(pick, mine[half])
        for q in range(FB):
            for i in range(tall // 8):
                wide[pl.ds(i * 64 + q, 8, stride=8), :] = part[
                    i * 8:(i + 1) * 8, q * LANE:(q + 1) * LANE
                ]
        for i in range(held):
            bufs[half][t, i] = wide[pl.ds(i * 8, 8), :].astype(jnp.bfloat16)

    count = chan.shape[1]
    flats = [b.reshape(b.shape[0] * held, 8, LANE) for b in bufs]

    def template(half, k):
        zr = [jnp.zeros((8, LANE), jnp.float32)] * 2
        zi = [jnp.zeros((8, LANE), jnp.float32)] * 2
        for j in range(CH):
            xv = flats[half][index[j, k]].astype(jnp.float32)
            uv = u[j * count + k].astype(jnp.float32)
            ur, ui = uv[:8], uv[8:]
            a = j % 2
            if half == 0:
                zr[a] = zr[a] + ur * xv
                zi[a] = zi[a] + ui * xv
            else:
                zr[a] = zr[a] + ui * xv
                zi[a] = zi[a] - ur * xv
        at = pl.ds(pl.multiple_of(k * SLOT, SLOT), 8)
        more = pl.ds(pl.multiple_of(k * SLOT + 8, 8), 8)
        if half == 0:
            z[at, :] = zr[0] + zr[1]
            z[more, :] = zi[0] + zi[1]
        else:
            z[at, :] = (z[at, :] + (zr[0] + zr[1])) * weight[...]
            z[more, :] = (z[more, :] + (zi[0] + zi[1])) * weight[...]

    def stack(half, first, last):
        def two(i, carry):
            template(half, 2 * i)
            template(half, 2 * i + 1)
            return carry

        lax.fori_loop(first // 2, last // 2, two, 0)

    c, s = gathers
    q4 = count // 4
    templates(0, 5)
    table_out.wait()
    compact(0)
    c.start()
    templates(5, 7)
    c.first()
    templates(7, 8)
    c.second()
    templates(8, 10)
    compact(1)
    s.start()
    templates(10, 12)
    c.third()
    templates(12, 13)
    s.first()
    c.fourth()
    templates(13, 15)
    s.second()
    c.finish()
    for f in fetches[10:]:
        f.wait()
    stack(0, 0, q4)
    s.third()
    stack(0, q4, 2 * q4)
    s.fourth()
    stack(0, 2 * q4, 4 * q4)
    s.finish()
    stack(1, 0, count)
    for q in range(QB):
        for i in range(count // 16):
            halves = [
                z[pl.ds((i * 16 + 8 * h) * SLOT + sub(q), 8, stride=SLOT), :] for h in range(2)
            ]
            packed[pl.ds(i * 16, 16), q * LANE:(q + 1) * LANE] = jnp.concatenate(
                halves, axis=0
            ).astype(jnp.bfloat16)
    out_ref[...] = dot(packed[...], inverse[...])

    for half in range(2):
        for move in moves[half]:
            move.wait_send()
        gathers[half].drain()


def matched(raw, fir, ids, channels, shifts, taps, wins, tmpls, held):
    count = taps.shape[2]
    slots, length = raw.shape
    pieces = length // SPAN
    tall = -(-held // 16) * 16
    forward = forward_table()
    args = (
        raw, fir.reshape(1, -1), ids.reshape(-1, LANE), channels, shifts, taps,
        jnp.asarray(np.stack([forward[:, :NF], forward[:, NF:]])), jnp.asarray(forward[:TL]), jnp.asarray(phase_table()),
        jnp.asarray(weight_tile()), jnp.asarray(inverse_table()),
    )
    smem = (4,)
    staged = [
        (pltpu.SMEM if i in smem else pltpu.VMEM)(a.shape, a.dtype) for i, a in enumerate(args)
    ]
    dma = pltpu.SemaphoreType.DMA
    return pl.pallas_call(
        functools.partial(match_kernel, wins),
        out_shape=jax.ShapeDtypeStruct((count, WIN_DEV), jnp.float32),
        in_specs=[pl.BlockSpec(memory_space=pl.ANY)] * len(args),
        out_specs=pl.BlockSpec(memory_space=pltpu.VMEM),
        scratch_shapes=staged + [
            pltpu.VMEM((8, 3 * LANE), jnp.float32),
            pltpu.VMEM((pieces * slots, 3 * LANE), jnp.bfloat16),
            pltpu.VMEM(((pieces + FB) * slots, LANE), jnp.bfloat16),
            pltpu.VMEM((wins * slots, NS), jnp.bfloat16),
            pltpu.VMEM((8, wins * slots), jnp.float32),
            pltpu.VMEM(channels.shape, jnp.int32),
            pltpu.SMEM(channels.shape, jnp.int32),
            pltpu.VMEM((2, wins * slots, NF), jnp.bfloat16),
            pltpu.VMEM((2, wins * slots, NF), jnp.bfloat16),
            pltpu.VMEM((tall * 8, LANE), jnp.float32),
            pltpu.VMEM((tmpls, held, 8, LANE), jnp.bfloat16),
            pltpu.VMEM((tmpls, held, 8, LANE), jnp.bfloat16),
            pltpu.VMEM((count * CH, SLOT, LANE), jnp.bfloat16),
            pltpu.VMEM((JB * count * SLOT, LANE), jnp.float32),
            pltpu.VMEM((count * SLOT, LANE), jnp.float32),
            pltpu.VMEM((count, NS), jnp.bfloat16),
            dma((len(args) + 2,)),
            dma((wins - 1,)), dma((wins - 1,)), dma((wins - 1,)), dma((wins - 1,)),
            dma((37,)), dma((37,)), dma((37,)), dma((37,)),
        ],
        compiler_params=pltpu.CompilerParams(
            vmem_limit_bytes=62 * MIB, collective_id=0, has_side_effects=True
        ),
        name="matched",
    )(*args)


def on_device(raw, ids, fir, taps, channels, shifts):
    wins = lax.axis_size("win")
    tmpls = lax.axis_size("tmpl")
    held = 3 * SLOTS * wins // 5
    return matched(
        raw, fir, ids, channels.T, shifts.T, jnp.transpose(taps, (1, 2, 0)), wins, tmpls, held
    )


def solution(mesh):
    return jax.shard_map(
        on_device,
        mesh=mesh,
        in_specs=(
            P(("win", "tmpl"), None),
            P(),
            P(),
            P("tmpl", None, None),
            P("tmpl", None),
            P("tmpl", None),
        ),
        out_specs=P("tmpl", "win"),
        check_vma=False,
    )
```

```python
import functools
import math

import jax
import jax.numpy as jnp
import numpy as np
from jax import lax
from jax.experimental import pallas as pl
from jax.experimental.pallas import tpu as pltpu
from jax.sharding import PartitionSpec as P

WIN_DEV = 1024
TL = 400
CH = 30
DEC = 2
NTAP = 64
MOVE = 256
NS = 1792
NF = 896
LANE = 128
FB = NF // LANE
QB = 2 * FB
SLOT = 16
SPAN = DEC * LANE
SLOTS = 16
TMPL = 16
CUT_C = 61
CUT_S = 61
MIB = 1 << 20


def cos_sin(rows, columns):
    angle = (np.arange(rows)[:, None] * np.arange(columns)[None, :] % NS) * (2.0 * math.pi / NS)
    return np.cos(angle), np.sin(angle)


def forward_table():
    c, s = cos_sin(NS, NF)
    return np.concatenate([c, s], axis=1).astype(jnp.bfloat16)


def inverse_table():
    c, s = cos_sin(NF, WIN_DEV)
    return np.concatenate([c, -s], axis=0).astype(jnp.bfloat16)


def phase_table():
    out = np.zeros((MOVE, 2, 8, LANE), np.float32)
    c, s = cos_sin(MOVE, NF)
    out[:, 0, :FB] = c.reshape(MOVE, FB, LANE)
    out[:, 1, :FB] = s.reshape(MOVE, FB, LANE)
    return out.reshape(MOVE, SLOT, LANE)


def weight_tile():
    w = np.full((NF,), 2.0 / (CH * NS), np.float32)
    w[0] = 1.0 / (CH * NS)
    out = np.zeros((8, LANE), np.float32)
    out[:FB] = w.reshape(FB, LANE)
    return out


def dot(a, b, dims=((1,), (0,))):
    return lax.dot_general(a, b, (dims, ((), ())), preferred_element_type=jnp.float32)


def plan(ids_ref, chan_ref, index_ref, rank_ref, held, high):
    ids = ids_ref[...]
    count, lanes = ids.shape
    group = lanes // SLOTS
    per = TMPL // group
    live = ids >= 0
    livef = live.astype(jnp.float32).astype(jnp.bfloat16)
    la = lax.broadcasted_iota(jnp.int32, (lanes, lanes), 0)
    lb = lax.broadcasted_iota(jnp.int32, (lanes, lanes), 1)
    same = (la // SLOTS) == (lb // SLOTS)
    total = dot(livef, same.astype(jnp.float32).astype(jnp.bfloat16)).astype(jnp.bfloat16)
    upto = dot(livef, (same & (la <= lb)).astype(jnp.float32).astype(jnp.bfloat16))
    ra = lax.broadcasted_iota(jnp.int32, (count, count), 0)
    rb = lax.broadcasted_iota(jnp.int32, (count, count), 1)
    before = ((ra % per) == (rb % per)) & (rb < ra)
    rank = upto + dot(before.astype(jnp.float32).astype(jnp.bfloat16), total)
    rank = jnp.where(live, rank, 0.0)
    row = lax.broadcasted_iota(jnp.int32, (count, lanes), 0)
    lane = lax.broadcasted_iota(jnp.int32, (count, lanes), 1)
    column = (row % per) * group + lane // SLOTS
    place = column * held + rank.astype(jnp.int32) - 1

    slots = count // per * SLOTS
    me = lax.axis_index("tmpl")
    sa = lax.broadcasted_iota(jnp.int32, (lanes, slots), 0)
    sb = lax.broadcasted_iota(jnp.int32, (lanes, slots), 1)
    chosen = sa == (me % group) * SLOTS + (sb % SLOTS)
    mine = dot(rank.astype(jnp.bfloat16), chosen.astype(jnp.float32).astype(jnp.bfloat16))
    oa = lax.broadcasted_iota(jnp.int32, (count, slots), 0)
    ob = lax.broadcasted_iota(jnp.int32, (count, slots), 1)
    mine = jnp.where(oa == (ob // SLOTS) * per + me // group, mine, 0.0)
    rank_ref[...] = jnp.broadcast_to(jnp.sum(mine, axis=0, keepdims=True), rank_ref.shape)

    hi_iota = lax.broadcasted_iota(jnp.int32, (high, lanes), 0)
    lo_iota = lax.broadcasted_iota(jnp.int32, (LANE, lanes), 0)
    hi_sum = jnp.zeros((high, LANE), jnp.float32)
    lo_sum = jnp.zeros((high, LANE), jnp.float32)
    for r in range(count):
        label = ids[r:r + 1]
        at = place[r:r + 1]
        hit = hi_iota == (label >> 7)
        hi = jnp.where(hit, (at >> 6).astype(jnp.float32), 0.0).astype(jnp.bfloat16)
        lo = jnp.where(hit, (at & 63).astype(jnp.float32), 0.0).astype(jnp.bfloat16)
        low = (lo_iota == (label & 127)).astype(jnp.float32).astype(jnp.bfloat16)
        hi_sum = hi_sum + dot(hi, low, ((1,), (1,)))
        lo_sum = lo_sum + dot(lo, low, ((1,), (1,)))
    both = jnp.concatenate([hi_sum, lo_sum], axis=0).astype(jnp.bfloat16)
    for j in range(chan_ref.shape[0]):
        name = chan_ref[j:j + 1, :]
        low = (lo_iota == (name & 127)).astype(jnp.float32).astype(jnp.bfloat16)
        got = dot(both, low)
        hit = hi_iota == (name >> 7)
        hi = jnp.sum(jnp.where(hit, got[:high], 0.0), axis=0, keepdims=True)
        lo = jnp.sum(jnp.where(hit, got[high:], 0.0), axis=0, keepdims=True)
        found = hi.astype(jnp.int32) * 64 + lo.astype(jnp.int32)
        index_ref[j:j + 1, :] = jnp.clip(found, 0, TMPL * held - 1)


def sub(q):
    return q if q < FB else q + 1


JB = 2
UNROLL = 32
MESH = pl.DeviceIdType.MESH


def filtered_tiles(raw, fir, seg, filt, tile, taps_wide):
    rows = raw.shape[0]
    pieces = raw.shape[1] // SPAN
    wins = tile.shape[0] // rows
    per = pieces // wins
    taps_wide[...] = jnp.zeros_like(taps_wide)
    taps_wide[0:1, 0:NTAP] = fir[...].astype(jnp.float32)
    wide = jnp.broadcast_to(taps_wide[0:1, :], (LANE, 3 * LANE))
    band = pltpu.roll(wide, 0, 1, stride=DEC, stride_axis=0).astype(jnp.bfloat16)
    for b in range(pieces):
        here = pl.ds(b * rows, rows)
        seg[here, :SPAN] = raw[:, b * SPAN:(b + 1) * SPAN]
        if b + 1 < pieces:
            seg[here, SPAN:] = raw[:, (b + 1) * SPAN:(b + 1) * SPAN + LANE]
        else:
            seg[here, SPAN:] = jnp.zeros((rows, LANE), jnp.bfloat16)
    filt[pl.ds(0, pieces * rows), :] = dot(seg[...], band, ((1,), (1,))).astype(jnp.bfloat16)
    filt[pl.ds(pieces * rows, FB * rows), :] = jnp.zeros((FB * rows, LANE), jnp.bfloat16)
    for w in range(wins):
        for q in range(QB):
            tile[pl.ds(w * rows, rows), q * LANE:(q + 1) * LANE] = filt[
                pl.ds((w * per + q) * rows, rows), :
            ]
    values = tile[...].astype(jnp.float32)
    return lax.rsqrt(jnp.mean(values * values, axis=1, keepdims=True) + 1e-05)


def template_spectra(first, last, shift_ref, taps, head, phase, u, spread):
    count = taps.shape[2]
    many = JB * count
    turns = count // UNROLL

    def one(step, carry):
        lhs = jnp.concatenate([taps[step * JB + j].T for j in range(JB)], axis=0)
        for c in range(NS // SPAN):
            spec = dot(lhs, head[:, c * SPAN:(c + 1) * SPAN])
            for h in range(2):
                for g in range(many // 8):
                    spread[pl.ds((g * QB + 2 * c + h) * 8, 8), :] = spec[
                        g * 8:(g + 1) * 8, h * LANE:(h + 1) * LANE
                    ]

        def rows(i, inner):
            for r in range(UNROLL):
                row = i * UNROLL + r
                base = i * (UNROLL // 8 * QB * 8) + (r // 8) * QB * 8 + r % 8
                tc = spread[pl.ds(base, 8, stride=8), :]
                ts = spread[pl.ds(base + FB * 8, 8, stride=8), :]
                s = shift_ref[step * JB + i // turns, (i % turns) * UNROLL + r]
                pc = phase[s, 0:8, :]
                ps = phase[s, 8:16, :]
                u[step * many + row] = jnp.concatenate(
                    [tc * pc - ts * ps, ts * pc + tc * ps], axis=0
                ).astype(jnp.bfloat16)
            return inner

        lax.fori_loop(0, many // UNROLL, rows, 0)
        return carry

    lax.fori_loop(first, last, one, 0)


class Gather:
    def __init__(self, buf, cut, send_sem, recv_sem):
        t = lax.axis_index("tmpl")
        zl, x, c = t // 8, (t // 2) % 4, t % 2
        self.buf, self.ss, self.rs = buf, send_sem, recv_sem
        self.zl, self.x, self.zo = zl, x, 1 - zl
        self.xp, self.xm, self.x2 = lax.rem(x + 1, 4), lax.rem(x + 3, 4), lax.rem(x + 2, 4)
        self.ix = lambda a, b: (a * 4 + b) * 2 + c
        self.ox = lambda a, b: (a * 4 + b) * 2 + 1 - c
        self.up, self.down = self.ix(zl, self.xp), self.ix(zl, self.xm)
        self.over, self.beside = self.ix(self.zo, x), self.ox(zl, x)
        self.me = self.ix(zl, x)
        held = buf.shape[1]
        rest = held - cut
        self.low, self.high, self.whole = (0, cut), (cut, rest), (0, held)
        self.low1, self.low2 = (0, cut // 2), (cut // 2, cut - cut // 2)
        self.high1, self.high2 = (cut, rest // 2), (cut + rest // 2, rest - rest // 2)
        self.sends, self.last, self.wait = [], [], {}

    def copy(self, of, seg, to, k):
        ref = self.buf.at[of, pl.ds(seg[0], seg[1])]
        return pltpu.make_async_remote_copy(
            src_ref=ref, dst_ref=ref, send_sem=self.ss.at[k], recv_sem=self.rs.at[k],
            device_id={"tmpl": to}, device_id_type=MESH,
        )

    def send(self, name, of, seg, to, back):
        if seg[1]:
            k = len(self.sends)
            s = self.copy(of, seg, to, k)
            s.start()
            self.sends.append(s)
            self.wait[name] = self.copy(back, seg, to, k)

    def relay(self, a, b, seg):
        name = "beside" + str(len(self.last))
        self.send(name, self.ix(a, b), seg, self.beside, self.ox(a, b))
        if name in self.wait:
            self.last.append(self.wait[name])

    def came(self, name):
        if name in self.wait:
            self.wait[name].wait_recv()

    def start(self):
        ix, zl, zo, x, xm, xp = self.ix, self.zl, self.zo, self.x, self.xm, self.xp
        self.send("z high", self.me, self.high, self.over, ix(zo, x))
        self.send("up low", self.me, self.low, self.up, ix(zl, xm))
        self.send("down low", self.me, self.low, self.down, ix(zl, xp))
        self.send("up high", self.me, self.high, self.up, ix(zl, xm))
        self.send("down high", self.me, self.high, self.down, ix(zl, xp))
        self.send("z low", self.me, self.low, self.over, ix(zo, x))
        self.relay(zl, x, self.whole)

    def first(self):
        ix, zl, zo, x, xm, xp, x2 = self.ix, self.zl, self.zo, self.x, self.xm, self.xp, self.x2
        self.came("up low")
        self.send("up low1", ix(zl, xm), self.low1, self.up, ix(zl, x2))
        self.send("z low m", ix(zl, xm), self.low, self.over, ix(zo, xm))
        self.relay(zl, xm, self.low)
        self.came("down low")
        self.send("down low2", ix(zl, xp), self.low2, self.down, ix(zl, x2))
        self.send("z low p", ix(zl, xp), self.low, self.over, ix(zo, xp))
        self.relay(zl, xp, self.low)
        self.came("z high")
        self.send("up z", ix(zo, x), self.high, self.up, ix(zo, xm))
        self.send("down z", ix(zo, x), self.high, self.down, ix(zo, xp))
        self.relay(zo, x, self.high)

    def second(self):
        ix, zl, zo, x, xm, xp, x2 = self.ix, self.zl, self.zo, self.x, self.xm, self.xp, self.x2
        self.came("up high")
        self.send("up high1", ix(zl, xm), self.high1, self.up, ix(zl, x2))
        self.relay(zl, xm, self.high)
        self.came("down high")
        self.send("down high2", ix(zl, xp), self.high2, self.down, ix(zl, x2))
        self.relay(zl, xp, self.high)
        self.came("z low")
        self.relay(zo, x, self.low)

    def third(self):
        ix, zl, zo, xm, xp, x2 = self.ix, self.zl, self.zo, self.xm, self.xp, self.x2
        self.came("up low1")
        self.send("z low1", ix(zl, x2), self.low1, self.over, ix(zo, x2))
        self.relay(zl, x2, self.low1)
        self.came("down low2")
        self.send("z low2", ix(zl, x2), self.low2, self.over, ix(zo, x2))
        self.relay(zl, x2, self.low2)
        self.came("up z")
        self.send("up z1", ix(zo, xm), self.high1, self.up, ix(zo, x2))
        self.relay(zo, xm, self.high)
        self.came("down z")
        self.send("down z2", ix(zo, xp), self.high2, self.down, ix(zo, x2))
        self.relay(zo, xp, self.high)

    def fourth(self):
        for name, a, b, seg in (
            ("z low m", self.zo, self.xm, self.low), ("z low p", self.zo, self.xp, self.low),
            ("up high1", self.zl, self.x2, self.high1), ("down high2", self.zl, self.x2, self.high2),
        ):
            self.came(name)
            self.relay(a, b, seg)

    def finish(self):
        for name, a, b, seg in (
            ("z low1", self.zo, self.x2, self.low1), ("z low2", self.zo, self.x2, self.low2),
            ("up z1", self.zo, self.x2, self.high1), ("down z2", self.zo, self.x2, self.high2),
        ):
            self.came(name)
            self.relay(a, b, seg)
        for r in self.last:
            r.wait_recv()

    def drain(self):
        for s in self.sends:
            s.wait_send()


def match_kernel(
    wins,
    raw_hbm, fir_hbm, ids_hbm, chan_hbm, shift_hbm, taps_hbm, table_hbm, head_hbm, phase_hbm,
    weight_hbm, inverse_hbm,
    out_ref,
    raw, fir, ids, chan, shift, taps, table, head, phase, weight, inverse,
    fir_wide, seg, filt, tile, rank, index_v, index, spec, mine, wide, buf_c, buf_s, u, spread, z,
    packed, fetch_sem, a_send, a_recv, b_send, b_recv, c_send, c_recv, s_send, s_recv,
):
    slots = raw.shape[0]
    w = lax.axis_index("win")
    t = lax.axis_index("tmpl")
    held = buf_c.shape[1]
    moves_of = ((a_send, a_recv), (b_send, b_recv))
    bufs = (buf_c, buf_s)
    gathers = (
        Gather(buf_c, CUT_C, c_send, c_recv), Gather(buf_s, CUT_S, s_send, s_recv)
    )

    barrier = pltpu.get_barrier_semaphore()
    for d in range(1, wins):
        pl.semaphore_signal(
            barrier, inc=1, device_id={"win": lax.rem(w + d, wins)}, device_id_type=MESH
        )
    g = gathers[0]
    for d in (g.up, g.down, g.over, g.beside):
        pl.semaphore_signal(barrier, inc=1, device_id={"tmpl": d}, device_id_type=MESH)

    pairs = (
        (raw_hbm, raw), (fir_hbm, fir), (table_hbm.at[0], table.at[0]),
        (table_hbm.at[1], table.at[1]), (ids_hbm, ids), (chan_hbm, chan), (shift_hbm, shift),
        (taps_hbm, taps), (head_hbm, head), (phase_hbm, phase),
        (weight_hbm, weight), (inverse_hbm, inverse),
    )
    fetches = [
        pltpu.make_async_copy(a, b, fetch_sem.at[i]) for i, (a, b) in enumerate(pairs)
    ]
    for f in fetches[:7]:
        f.start()

    fetches[0].wait()
    fetches[1].wait()
    scale = filtered_tiles(raw, fir, seg, filt, tile, fir_wide)

    def block(ref, half, i):
        return ref.at[half, pl.ds(pl.multiple_of(i * slots, slots), slots)]

    own = pl.ds(pl.multiple_of(w * slots, slots), slots)
    moves = ([], [])

    def transform(half):
        fetches[2 + half].wait()
        spec[half] = (dot(tile[...], table[half]) * scale).astype(jnp.bfloat16)

    def spread_rows(half):
        for d in range(1, wins):
            to = lax.rem(w + d, wins)
            move = pltpu.make_async_remote_copy(
                src_ref=block(spec, half, to), dst_ref=block(mine, half, w),
                send_sem=moves_of[half][0].at[d - 1], recv_sem=moves_of[half][1].at[d - 1],
                device_id={"win": to}, device_id_type=MESH,
            )
            move.start()
            moves[half].append(move)
        mine[half, own, :] = spec[half, own, :]

    transform(0)
    pl.semaphore_wait(barrier, wins + 3)
    spread_rows(0)
    transform(1)
    for f in fetches[7:]:
        f.start()
    fetches[4].wait()
    fetches[5].wait()
    plan(ids, chan, index_v, rank, held, -(-held * TMPL // (8 * LANE)) * 8)
    table_out = pltpu.make_async_copy(index_v, index, fetch_sem.at[len(pairs)])
    table_out.start()
    for f in fetches[6:10]:
        f.wait()

    def templates(first, last):
        template_spectra(first, last, shift, taps, head, phase, u, spread)

    tall = wide.shape[0] // 8

    def compact(half):
        for move in moves[half]:
            move.wait_recv()
        order = lax.broadcasted_iota(jnp.int32, (tall, mine.shape[1]), 0).astype(jnp.float32) + 1.0
        pick = (order == rank[0:1, :]).astype(jnp.float32).astype(jnp.bfloat16)
        part = dot(pick, mine[half])
        for q in range(FB):
            for i in range(tall // 8):
                wide[pl.ds(i * 64 + q, 8, stride=8), :] = part[
                    i * 8:(i + 1) * 8, q * LANE:(q + 1) * LANE
                ]
        for i in range(held):
            bufs[half][t, i] = wide[pl.ds(i * 8, 8), :].astype(jnp.bfloat16)

    count = chan.shape[1]
    flats = [b.reshape(b.shape[0] * held, 8, LANE) for b in bufs]

    def template(half, k):
        zr = [jnp.zeros((8, LANE), jnp.float32)] * 2
        zi = [jnp.zeros((8, LANE), jnp.float32)] * 2
        for j in range(CH):
            xv = flats[half][index[j, k]].astype(jnp.float32)
            uv = u[j * count + k].astype(jnp.float32)
            ur, ui = uv[:8], uv[8:]
            a = j % 2
            if half == 0:
                zr[a] = zr[a] + ur * xv
                zi[a] = zi[a] + ui * xv
            else:
                zr[a] = zr[a] + ui * xv
                zi[a] = zi[a] - ur * xv
        at = pl.ds(pl.multiple_of(k * SLOT, SLOT), 8)
        more = pl.ds(pl.multiple_of(k * SLOT + 8, 8), 8)
        if half == 0:
            z[at, :] = zr[0] + zr[1]
            z[more, :] = zi[0] + zi[1]
        else:
            z[at, :] = (z[at, :] + (zr[0] + zr[1])) * weight[...]
            z[more, :] = (z[more, :] + (zi[0] + zi[1])) * weight[...]

    def stack(half, first, last):
        def two(i, carry):
            template(half, 2 * i)
            template(half, 2 * i + 1)
            return carry

        lax.fori_loop(first // 2, last // 2, two, 0)

    c, s = gathers
    q4 = count // 4
    templates(0,3)
    table_out.wait()
    compact(0)
    c.start()
    spread_rows(1)
    templates(3,5)
    c.first()
    templates(5,7)
    c.second()
    templates(7,9)
    compact(1)
    s.start()
    templates(9,11)
    c.third()
    templates(11,12)
    s.first()
    c.fourth()
    templates(12,15)
    s.second()
    c.finish()
    for f in fetches[10:]:
        f.wait()
    stack(0,0,q4)
    s.third()
    stack(0,q4,2*q4)
    s.fourth()
    stack(0,2*q4,4*q4)
    s.finish()
    stack(1, 0, count)
    for q in range(QB):
        for i in range(count // 16):
            halves = [
                z[pl.ds((i * 16 + 8 * h) * SLOT + sub(q), 8, stride=SLOT), :] for h in range(2)
            ]
            packed[pl.ds(i * 16, 16), q * LANE:(q + 1) * LANE] = jnp.concatenate(
                halves, axis=0
            ).astype(jnp.bfloat16)
    out_ref[...] = dot(packed[...], inverse[...])

    for half in range(2):
        for move in moves[half]:
            move.wait_send()
        gathers[half].drain()


def matched(raw, fir, ids, channels, shifts, taps, wins, tmpls, held):
    count = taps.shape[2]
    slots, length = raw.shape
    pieces = length // SPAN
    tall = -(-held // 16) * 16
    forward = forward_table()
    args = (
        raw, fir.reshape(1, -1), ids.reshape(-1, LANE), channels, shifts, taps,
        jnp.asarray(np.stack([forward[:, :NF], forward[:, NF:]])), jnp.asarray(forward[:TL]), jnp.asarray(phase_table()),
        jnp.asarray(weight_tile()), jnp.asarray(inverse_table()),
    )
    smem = (4,)
    staged = [
        (pltpu.SMEM if i in smem else pltpu.VMEM)(a.shape, a.dtype) for i, a in enumerate(args)
    ]
    dma = pltpu.SemaphoreType.DMA
    return pl.pallas_call(
        functools.partial(match_kernel, wins),
        out_shape=jax.ShapeDtypeStruct((count, WIN_DEV), jnp.float32),
        in_specs=[pl.BlockSpec(memory_space=pl.ANY)] * len(args),
        out_specs=pl.BlockSpec(memory_space=pltpu.VMEM),
        scratch_shapes=staged + [
            pltpu.VMEM((8, 3 * LANE), jnp.float32),
            pltpu.VMEM((pieces * slots, 3 * LANE), jnp.bfloat16),
            pltpu.VMEM(((pieces + FB) * slots, LANE), jnp.bfloat16),
            pltpu.VMEM((wins * slots, NS), jnp.bfloat16),
            pltpu.VMEM((8, wins * slots), jnp.float32),
            pltpu.VMEM(channels.shape, jnp.int32),
            pltpu.SMEM(channels.shape, jnp.int32),
            pltpu.VMEM((2, wins * slots, NF), jnp.bfloat16),
            pltpu.VMEM((2, wins * slots, NF), jnp.bfloat16),
            pltpu.VMEM((tall * 8, LANE), jnp.float32),
            pltpu.VMEM((tmpls, held, 8, LANE), jnp.bfloat16),
            pltpu.VMEM((tmpls, held, 8, LANE), jnp.bfloat16),
            pltpu.VMEM((count * CH, SLOT, LANE), jnp.bfloat16),
            pltpu.VMEM((JB * count * SLOT, LANE), jnp.float32),
            pltpu.VMEM((count * SLOT, LANE), jnp.float32),
            pltpu.VMEM((count, NS), jnp.bfloat16),
            dma((len(args) + 2,)),
            dma((wins - 1,)), dma((wins - 1,)), dma((wins - 1,)), dma((wins - 1,)),
            dma((37,)), dma((37,)), dma((37,)), dma((37,)),
        ],
        compiler_params=pltpu.CompilerParams(
            vmem_limit_bytes=62 * MIB, collective_id=0, has_side_effects=True
        ),
        name="matched",
    )(*args)


def on_device(raw, ids, fir, taps, channels, shifts):
    wins = lax.axis_size("win")
    tmpls = lax.axis_size("tmpl")
    held = 3 * SLOTS * wins // 5
    return matched(
        raw, fir, ids, channels.T, shifts.T, jnp.transpose(taps, (1, 2, 0)), wins, tmpls, held
    )


def solution(mesh):
    return jax.shard_map(
        on_device,
        mesh=mesh,
        in_specs=(
            P(("win", "tmpl"), None),
            P(),
            P(),
            P("tmpl", None, None),
            P("tmpl", None),
            P("tmpl", None),
        ),
        out_specs=P("tmpl", "win"),
        check_vma=False,
    )
```

```python
import functools
import math

import jax
import jax.numpy as jnp
import numpy as np
from jax import lax
from jax.experimental import pallas as pl
from jax.experimental.pallas import tpu as pltpu
from jax.sharding import PartitionSpec as P

WIN_DEV = 1024
TL = 400
CH = 30
DEC = 2
NTAP = 64
MOVE = 256
NS = 1792
NF = 896
LANE = 128
FB = NF // LANE
QB = 2 * FB
SLOT = 16
SPAN = DEC * LANE
SLOTS = 16
TMPL = 16
CUT_C = 61
CUT_S = 61
MIB = 1 << 20


def cos_sin(rows, columns):
    angle = (np.arange(rows)[:, None] * np.arange(columns)[None, :] % NS) * (2.0 * math.pi / NS)
    return np.cos(angle), np.sin(angle)


def forward_table():
    c, s = cos_sin(NS, NF)
    return np.concatenate([c, s], axis=1).astype(jnp.bfloat16)


def inverse_table():
    c, s = cos_sin(NF, WIN_DEV)
    return np.concatenate([c, -s], axis=0).astype(jnp.bfloat16)


def phase_table():
    out = np.zeros((MOVE, 2, 8, LANE), np.float32)
    c, s = cos_sin(MOVE, NF)
    out[:, 0, :FB] = c.reshape(MOVE, FB, LANE)
    out[:, 1, :FB] = s.reshape(MOVE, FB, LANE)
    return out.reshape(MOVE, SLOT, LANE)


def weight_tile():
    w = np.full((NF,), 2.0 / (CH * NS), np.float32)
    w[0] = 1.0 / (CH * NS)
    out = np.zeros((8, LANE), np.float32)
    out[:FB] = w.reshape(FB, LANE)
    return out


def dot(a, b, dims=((1,), (0,))):
    return lax.dot_general(a, b, (dims, ((), ())), preferred_element_type=jnp.float32)


def plan(ids_ref, chan_ref, index_ref, rank_ref, held, high):
    ids = ids_ref[...]
    count, lanes = ids.shape
    group = lanes // SLOTS
    per = TMPL // group
    live = ids >= 0
    livef = live.astype(jnp.float32).astype(jnp.bfloat16)
    la = lax.broadcasted_iota(jnp.int32, (lanes, lanes), 0)
    lb = lax.broadcasted_iota(jnp.int32, (lanes, lanes), 1)
    same = (la // SLOTS) == (lb // SLOTS)
    total = dot(livef, same.astype(jnp.float32).astype(jnp.bfloat16)).astype(jnp.bfloat16)
    upto = dot(livef, (same & (la <= lb)).astype(jnp.float32).astype(jnp.bfloat16))
    ra = lax.broadcasted_iota(jnp.int32, (count, count), 0)
    rb = lax.broadcasted_iota(jnp.int32, (count, count), 1)
    before = ((ra % per) == (rb % per)) & (rb < ra)
    rank = upto + dot(before.astype(jnp.float32).astype(jnp.bfloat16), total)
    rank = jnp.where(live, rank, 0.0)
    row = lax.broadcasted_iota(jnp.int32, (count, lanes), 0)
    lane = lax.broadcasted_iota(jnp.int32, (count, lanes), 1)
    column = (row % per) * group + lane // SLOTS
    place = column * held + rank.astype(jnp.int32) - 1

    slots = count // per * SLOTS
    me = lax.axis_index("tmpl")
    sa = lax.broadcasted_iota(jnp.int32, (lanes, slots), 0)
    sb = lax.broadcasted_iota(jnp.int32, (lanes, slots), 1)
    chosen = sa == (me % group) * SLOTS + (sb % SLOTS)
    mine = dot(rank.astype(jnp.bfloat16), chosen.astype(jnp.float32).astype(jnp.bfloat16))
    oa = lax.broadcasted_iota(jnp.int32, (count, slots), 0)
    ob = lax.broadcasted_iota(jnp.int32, (count, slots), 1)
    mine = jnp.where(oa == (ob // SLOTS) * per + me // group, mine, 0.0)
    rank_ref[...] = jnp.broadcast_to(jnp.sum(mine, axis=0, keepdims=True), rank_ref.shape)

    hi_iota = lax.broadcasted_iota(jnp.int32, (high, lanes), 0)
    lo_iota = lax.broadcasted_iota(jnp.int32, (LANE, lanes), 0)
    hi_sum = jnp.zeros((high, LANE), jnp.float32)
    lo_sum = jnp.zeros((high, LANE), jnp.float32)
    for r in range(count):
        label = ids[r:r + 1]
        at = place[r:r + 1]
        hit = hi_iota == (label >> 7)
        hi = jnp.where(hit, (at >> 6).astype(jnp.float32), 0.0).astype(jnp.bfloat16)
        lo = jnp.where(hit, (at & 63).astype(jnp.float32), 0.0).astype(jnp.bfloat16)
        low = (lo_iota == (label & 127)).astype(jnp.float32).astype(jnp.bfloat16)
        hi_sum = hi_sum + dot(hi, low, ((1,), (1,)))
        lo_sum = lo_sum + dot(lo, low, ((1,), (1,)))
    both = jnp.concatenate([hi_sum, lo_sum], axis=0).astype(jnp.bfloat16)
    for j in range(chan_ref.shape[0]):
        name = chan_ref[j:j + 1, :]
        low = (lo_iota == (name & 127)).astype(jnp.float32).astype(jnp.bfloat16)
        got = dot(both, low)
        hit = hi_iota == (name >> 7)
        hi = jnp.sum(jnp.where(hit, got[:high], 0.0), axis=0, keepdims=True)
        lo = jnp.sum(jnp.where(hit, got[high:], 0.0), axis=0, keepdims=True)
        found = hi.astype(jnp.int32) * 64 + lo.astype(jnp.int32)
        index_ref[j:j + 1, :] = jnp.clip(found, 0, TMPL * held - 1)


def sub(q):
    return q if q < FB else q + 1


JB = 2
UNROLL = 32
MESH = pl.DeviceIdType.MESH


def filtered_tiles(raw, fir, seg, filt, tile, taps_wide):
    rows = raw.shape[0]
    pieces = raw.shape[1] // SPAN
    wins = tile.shape[0] // rows
    per = pieces // wins
    taps_wide[...] = jnp.zeros_like(taps_wide)
    taps_wide[0:1, 0:NTAP] = fir[...].astype(jnp.float32)
    wide = jnp.broadcast_to(taps_wide[0:1, :], (LANE, 3 * LANE))
    band = pltpu.roll(wide, 0, 1, stride=DEC, stride_axis=0).astype(jnp.bfloat16)
    for b in range(pieces):
        here = pl.ds(b * rows, rows)
        seg[here, :SPAN] = raw[:, b * SPAN:(b + 1) * SPAN]
        if b + 1 < pieces:
            seg[here, SPAN:] = raw[:, (b + 1) * SPAN:(b + 1) * SPAN + LANE]
        else:
            seg[here, SPAN:] = jnp.zeros((rows, LANE), jnp.bfloat16)
    filt[pl.ds(0, pieces * rows), :] = dot(seg[...], band, ((1,), (1,))).astype(jnp.bfloat16)
    filt[pl.ds(pieces * rows, FB * rows), :] = jnp.zeros((FB * rows, LANE), jnp.bfloat16)
    for w in range(wins):
        for q in range(QB):
            tile[pl.ds(w * rows, rows), q * LANE:(q + 1) * LANE] = filt[
                pl.ds((w * per + q) * rows, rows), :
            ]
    values = tile[...].astype(jnp.float32)
    return lax.rsqrt(jnp.mean(values * values, axis=1, keepdims=True) + 1e-05)


def template_spectra(first, last, shift_ref, taps, head, phase, u, spread):
    count = taps.shape[2]
    many = JB * count
    turns = count // UNROLL

    def one(step, carry):
        lhs = jnp.concatenate([taps[step * JB + j].T for j in range(JB)], axis=0)
        for c in range(NS // SPAN):
            spec = dot(lhs, head[:, c * SPAN:(c + 1) * SPAN])
            for h in range(2):
                for g in range(many // 8):
                    spread[pl.ds((g * QB + 2 * c + h) * 8, 8), :] = spec[
                        g * 8:(g + 1) * 8, h * LANE:(h + 1) * LANE
                    ]

        def rows(i, inner):
            for r in range(UNROLL):
                row = i * UNROLL + r
                base = i * (UNROLL // 8 * QB * 8) + (r // 8) * QB * 8 + r % 8
                tc = spread[pl.ds(base, 8, stride=8), :]
                ts = spread[pl.ds(base + FB * 8, 8, stride=8), :]
                s = shift_ref[step * JB + i // turns, (i % turns) * UNROLL + r]
                pc = phase[s, 0:8, :]
                ps = phase[s, 8:16, :]
                u[step * many + row] = jnp.concatenate(
                    [tc * pc - ts * ps, ts * pc + tc * ps], axis=0
                ).astype(jnp.bfloat16)
            return inner

        lax.fori_loop(0, many // UNROLL, rows, 0)
        return carry

    lax.fori_loop(first, last, one, 0)


class Gather:
    def __init__(self, buf, cut, send_sem, recv_sem):
        t = lax.axis_index("tmpl")
        zl, x, c = t // 8, (t // 2) % 4, t % 2
        self.buf, self.ss, self.rs = buf, send_sem, recv_sem
        self.zl, self.x, self.zo = zl, x, 1 - zl
        self.xp, self.xm, self.x2 = lax.rem(x + 1, 4), lax.rem(x + 3, 4), lax.rem(x + 2, 4)
        self.ix = lambda a, b: (a * 4 + b) * 2 + c
        self.ox = lambda a, b: (a * 4 + b) * 2 + 1 - c
        self.up, self.down = self.ix(zl, self.xp), self.ix(zl, self.xm)
        self.over, self.beside = self.ix(self.zo, x), self.ox(zl, x)
        self.me = self.ix(zl, x)
        held = buf.shape[1]
        rest = held - cut
        self.low, self.high, self.whole = (0, cut), (cut, rest), (0, held)
        self.low1, self.low2 = (0, cut // 2), (cut // 2, cut - cut // 2)
        self.high1, self.high2 = (cut, rest // 2), (cut + rest // 2, rest - rest // 2)
        self.sends, self.last, self.wait = [], [], {}

    def copy(self, of, seg, to, k):
        ref = self.buf.at[of, pl.ds(seg[0], seg[1])]
        return pltpu.make_async_remote_copy(
            src_ref=ref, dst_ref=ref, send_sem=self.ss.at[k], recv_sem=self.rs.at[k],
            device_id={"tmpl": to}, device_id_type=MESH,
        )

    def send(self, name, of, seg, to, back):
        if seg[1]:
            k = len(self.sends)
            s = self.copy(of, seg, to, k)
            s.start()
            self.sends.append(s)
            self.wait[name] = self.copy(back, seg, to, k)

    def relay(self, a, b, seg):
        name = "beside" + str(len(self.last))
        self.send(name, self.ix(a, b), seg, self.beside, self.ox(a, b))
        if name in self.wait:
            self.last.append(self.wait[name])

    def came(self, name):
        if name in self.wait:
            self.wait[name].wait_recv()

    def start(self):
        ix, zl, zo, x, xm, xp = self.ix, self.zl, self.zo, self.x, self.xm, self.xp
        self.send("z high", self.me, self.high, self.over, ix(zo, x))
        self.send("up low", self.me, self.low, self.up, ix(zl, xm))
        self.send("down low", self.me, self.low, self.down, ix(zl, xp))
        self.send("up high", self.me, self.high, self.up, ix(zl, xm))
        self.send("down high", self.me, self.high, self.down, ix(zl, xp))
        self.send("z low", self.me, self.low, self.over, ix(zo, x))
        self.relay(zl, x, self.whole)

    def first(self):
        ix, zl, zo, x, xm, xp, x2 = self.ix, self.zl, self.zo, self.x, self.xm, self.xp, self.x2
        self.came("up low")
        self.send("up low1", ix(zl, xm), self.low1, self.up, ix(zl, x2))
        self.send("z low m", ix(zl, xm), self.low, self.over, ix(zo, xm))
        self.relay(zl, xm, self.low)
        self.came("down low")
        self.send("down low2", ix(zl, xp), self.low2, self.down, ix(zl, x2))
        self.send("z low p", ix(zl, xp), self.low, self.over, ix(zo, xp))
        self.relay(zl, xp, self.low)
        self.came("z high")
        self.send("up z", ix(zo, x), self.high, self.up, ix(zo, xm))
        self.send("down z", ix(zo, x), self.high, self.down, ix(zo, xp))
        self.relay(zo, x, self.high)

    def second(self):
        ix, zl, zo, x, xm, xp, x2 = self.ix, self.zl, self.zo, self.x, self.xm, self.xp, self.x2
        self.came("up high")
        self.send("up high1", ix(zl, xm), self.high1, self.up, ix(zl, x2))
        self.relay(zl, xm, self.high)
        self.came("down high")
        self.send("down high2", ix(zl, xp), self.high2, self.down, ix(zl, x2))
        self.relay(zl, xp, self.high)
        self.came("z low")
        self.relay(zo, x, self.low)

    def third(self):
        ix, zl, zo, xm, xp, x2 = self.ix, self.zl, self.zo, self.xm, self.xp, self.x2
        self.came("up low1")
        self.send("z low1", ix(zl, x2), self.low1, self.over, ix(zo, x2))
        self.relay(zl, x2, self.low1)
        self.came("down low2")
        self.send("z low2", ix(zl, x2), self.low2, self.over, ix(zo, x2))
        self.relay(zl, x2, self.low2)
        self.came("up z")
        self.send("up z1", ix(zo, xm), self.high1, self.up, ix(zo, x2))
        self.relay(zo, xm, self.high)
        self.came("down z")
        self.send("down z2", ix(zo, xp), self.high2, self.down, ix(zo, x2))
        self.relay(zo, xp, self.high)

    def fourth(self):
        for name, a, b, seg in (
            ("z low m", self.zo, self.xm, self.low), ("z low p", self.zo, self.xp, self.low),
            ("up high1", self.zl, self.x2, self.high1), ("down high2", self.zl, self.x2, self.high2),
        ):
            self.came(name)
            self.relay(a, b, seg)

    def finish(self):
        for name, a, b, seg in (
            ("z low1", self.zo, self.x2, self.low1), ("z low2", self.zo, self.x2, self.low2),
            ("up z1", self.zo, self.x2, self.high1), ("down z2", self.zo, self.x2, self.high2),
        ):
            self.came(name)
            self.relay(a, b, seg)
        for r in self.last:
            r.wait_recv()

    def drain(self):
        for s in self.sends:
            s.wait_send()


def match_kernel(
    wins,
    raw_hbm, fir_hbm, ids_hbm, chan_hbm, shift_hbm, taps_hbm, table_hbm, head_hbm, phase_hbm,
    weight_hbm, inverse_hbm,
    out_ref,
    raw, fir, ids, chan, shift, taps, table, head, phase, weight, inverse,
    fir_wide, seg, filt, tile, rank, index_v, index, spec, mine, wide, buf_c, buf_s, u, spread, z,
    packed, fetch_sem, a_send, a_recv, b_send, b_recv, c_send, c_recv, s_send, s_recv,
):
    slots = raw.shape[0]
    w = lax.axis_index("win")
    t = lax.axis_index("tmpl")
    held = buf_c.shape[1]
    moves_of = ((a_send, a_recv), (b_send, b_recv))
    bufs = (buf_c, buf_s)
    gathers = (
        Gather(buf_c, CUT_C, c_send, c_recv), Gather(buf_s, CUT_S, s_send, s_recv)
    )

    barrier = pltpu.get_barrier_semaphore()
    for d in range(1, wins):
        pl.semaphore_signal(
            barrier, inc=1, device_id={"win": lax.rem(w + d, wins)}, device_id_type=MESH
        )
    g = gathers[0]
    for d in (g.up, g.down, g.over, g.beside):
        pl.semaphore_signal(barrier, inc=1, device_id={"tmpl": d}, device_id_type=MESH)

    pairs = (
        (raw_hbm, raw), (fir_hbm, fir), (table_hbm.at[0], table.at[0]),
        (table_hbm.at[1], table.at[1]), (ids_hbm, ids), (chan_hbm, chan), (shift_hbm, shift),
        (taps_hbm, taps), (head_hbm, head), (phase_hbm, phase),
        (weight_hbm, weight), (inverse_hbm, inverse),
    )
    fetches = [
        pltpu.make_async_copy(a, b, fetch_sem.at[i]) for i, (a, b) in enumerate(pairs)
    ]
    for f in fetches[:7]:
        f.start()

    fetches[0].wait()
    fetches[1].wait()
    scale = filtered_tiles(raw, fir, seg, filt, tile, fir_wide)

    def block(ref, half, i):
        return ref.at[half, pl.ds(pl.multiple_of(i * slots, slots), slots)]

    own = pl.ds(pl.multiple_of(w * slots, slots), slots)
    moves = ([], [])

    def transform(half):
        fetches[2 + half].wait()
        spec[half] = (dot(tile[...], table[half]) * scale).astype(jnp.bfloat16)

    def spread_rows(half):
        for d in range(1, wins):
            to = lax.rem(w + d, wins)
            move = pltpu.make_async_remote_copy(
                src_ref=block(spec, half, to), dst_ref=block(mine, half, w),
                send_sem=moves_of[half][0].at[d - 1], recv_sem=moves_of[half][1].at[d - 1],
                device_id={"win": to}, device_id_type=MESH,
            )
            move.start()
            moves[half].append(move)
        mine[half, own, :] = spec[half, own, :]

    transform(0)
    pl.semaphore_wait(barrier, wins + 3)
    spread_rows(0)
    transform(1)
    for f in fetches[7:]:
        f.start()
    fetches[4].wait()
    fetches[5].wait()
    plan(ids, chan, index_v, rank, held, -(-held * TMPL // (8 * LANE)) * 8)
    table_out = pltpu.make_async_copy(index_v, index, fetch_sem.at[len(pairs)])
    table_out.start()
    for f in fetches[6:10]:
        f.wait()

    def templates(first, last):
        template_spectra(first, last, shift, taps, head, phase, u, spread)

    tall = wide.shape[0] // 8

    def compact(half):
        for move in moves[half]:
            move.wait_recv()
        order = lax.broadcasted_iota(jnp.int32, (tall, mine.shape[1]), 0).astype(jnp.float32) + 1.0
        pick = (order == rank[0:1, :]).astype(jnp.float32).astype(jnp.bfloat16)
        part = dot(pick, mine[half])
        for q in range(FB):
            for i in range(tall // 8):
                wide[pl.ds(i * 64 + q, 8, stride=8), :] = part[
                    i * 8:(i + 1) * 8, q * LANE:(q + 1) * LANE
                ]
        for i in range(held):
            bufs[half][t, i] = wide[pl.ds(i * 8, 8), :].astype(jnp.bfloat16)

    count = chan.shape[1]
    flats = [b.reshape(b.shape[0] * held, 8, LANE) for b in bufs]

    def template(half, k):
        zr = [jnp.zeros((8, LANE), jnp.float32)] * 2
        zi = [jnp.zeros((8, LANE), jnp.float32)] * 2
        for j in range(CH):
            xv = flats[half][index[j, k]].astype(jnp.float32)
            uv = u[j * count + k].astype(jnp.float32)
            ur, ui = uv[:8], uv[8:]
            a = j % 2
            if half == 0:
                zr[a] = zr[a] + ur * xv
                zi[a] = zi[a] + ui * xv
            else:
                zr[a] = zr[a] + ui * xv
                zi[a] = zi[a] - ur * xv
        at = pl.ds(pl.multiple_of(k * SLOT, SLOT), 8)
        more = pl.ds(pl.multiple_of(k * SLOT + 8, 8), 8)
        if half == 0:
            z[at, :] = zr[0] + zr[1]
            z[more, :] = zi[0] + zi[1]
        else:
            z[at, :] = (z[at, :] + (zr[0] + zr[1])) * weight[...]
            z[more, :] = (z[more, :] + (zi[0] + zi[1])) * weight[...]

    def stack(half, first, last):
        def four(i, carry):
            for k in range(4):
                template(half, 4 * i + k)
            return carry

        lax.fori_loop(first // 4, last // 4, four, 0)

    c, s = gathers
    q4 = count // 4
    templates(0,3)
    table_out.wait()
    compact(0)
    c.start()
    spread_rows(1)
    templates(3,5)
    c.first()
    templates(5,7)
    c.second()
    templates(7,9)
    compact(1)
    s.start()
    templates(9,11)
    c.third()
    templates(11,12)
    s.first()
    c.fourth()
    templates(12,15)
    s.second()
    c.finish()
    for f in fetches[10:]:
        f.wait()
    stack(0,0,q4)
    s.third()
    stack(0,q4,2*q4)
    s.fourth()
    stack(0,2*q4,4*q4)
    s.finish()
    stack(1, 0, count)
    for q in range(QB):
        for i in range(count // 16):
            halves = [
                z[pl.ds((i * 16 + 8 * h) * SLOT + sub(q), 8, stride=SLOT), :] for h in range(2)
            ]
            packed[pl.ds(i * 16, 16), q * LANE:(q + 1) * LANE] = jnp.concatenate(
                halves, axis=0
            ).astype(jnp.bfloat16)
    out_ref[...] = dot(packed[...], inverse[...])

    for half in range(2):
        for move in moves[half]:
            move.wait_send()
        gathers[half].drain()


def matched(raw, fir, ids, channels, shifts, taps, wins, tmpls, held):
    count = taps.shape[2]
    slots, length = raw.shape
    pieces = length // SPAN
    tall = -(-held // 16) * 16
    forward = forward_table()
    args = (
        raw, fir.reshape(1, -1), ids.reshape(-1, LANE), channels, shifts, taps,
        jnp.asarray(np.stack([forward[:, :NF], forward[:, NF:]])), jnp.asarray(forward[:TL]), jnp.asarray(phase_table()),
        jnp.asarray(weight_tile()), jnp.asarray(inverse_table()),
    )
    smem = (4,)
    staged = [
        (pltpu.SMEM if i in smem else pltpu.VMEM)(a.shape, a.dtype) for i, a in enumerate(args)
    ]
    dma = pltpu.SemaphoreType.DMA
    return pl.pallas_call(
        functools.partial(match_kernel, wins),
        out_shape=jax.ShapeDtypeStruct((count, WIN_DEV), jnp.float32),
        in_specs=[pl.BlockSpec(memory_space=pl.ANY)] * len(args),
        out_specs=pl.BlockSpec(memory_space=pltpu.VMEM),
        scratch_shapes=staged + [
            pltpu.VMEM((8, 3 * LANE), jnp.float32),
            pltpu.VMEM((pieces * slots, 3 * LANE), jnp.bfloat16),
            pltpu.VMEM(((pieces + FB) * slots, LANE), jnp.bfloat16),
            pltpu.VMEM((wins * slots, NS), jnp.bfloat16),
            pltpu.VMEM((8, wins * slots), jnp.float32),
            pltpu.VMEM(channels.shape, jnp.int32),
            pltpu.SMEM(channels.shape, jnp.int32),
            pltpu.VMEM((2, wins * slots, NF), jnp.bfloat16),
            pltpu.VMEM((2, wins * slots, NF), jnp.bfloat16),
            pltpu.VMEM((tall * 8, LANE), jnp.float32),
            pltpu.VMEM((tmpls, held, 8, LANE), jnp.bfloat16),
            pltpu.VMEM((tmpls, held, 8, LANE), jnp.bfloat16),
            pltpu.VMEM((count * CH, SLOT, LANE), jnp.bfloat16),
            pltpu.VMEM((JB * count * SLOT, LANE), jnp.float32),
            pltpu.VMEM((count * SLOT, LANE), jnp.float32),
            pltpu.VMEM((count, NS), jnp.bfloat16),
            dma((len(args) + 2,)),
            dma((wins - 1,)), dma((wins - 1,)), dma((wins - 1,)), dma((wins - 1,)),
            dma((37,)), dma((37,)), dma((37,)), dma((37,)),
        ],
        compiler_params=pltpu.CompilerParams(
            vmem_limit_bytes=62 * MIB, collective_id=0, has_side_effects=True
        ),
        name="matched",
    )(*args)


def on_device(raw, ids, fir, taps, channels, shifts):
    wins = lax.axis_size("win")
    tmpls = lax.axis_size("tmpl")
    held = 3 * SLOTS * wins // 5
    return matched(
        raw, fir, ids, channels.T, shifts.T, jnp.transpose(taps, (1, 2, 0)), wins, tmpls, held
    )


def solution(mesh):
    return jax.shard_map(
        on_device,
        mesh=mesh,
        in_specs=(
            P(("win", "tmpl"), None),
            P(),
            P(),
            P("tmpl", None, None),
            P("tmpl", None),
            P("tmpl", None),
        ),
        out_specs=P("tmpl", "win"),
        check_vma=False,
    )
```
